256 devices in a mesh: ex: 2 (over core), slab: 128 (over z, y, x).
Axes of the slice: x: 4, y: 4, z: 8, core: 2. Of those that a mesh axis runs over, the one named last changes fastest.
Arguments:
- volume: bfloat16 [2, 16, 128, 32, 128], P('ex', None, 'slab'), may hold values from -6 to 6
- cotangent: bfloat16 [2, 16, 128, 32, 128], P('ex', None, 'slab')
- gate_mask: int32 [2, 2, 128, 32, 128], P('ex', None, 'slab'), may hold values 0 or 1
- loss_scale: float32 [2], P('ex'), may hold values from 0.05 to 5
- canary: int32 [2], P('ex'), may hold values from 0 to 15
- kernels: bfloat16 [2, 32, 432], replicated, may hold values from -0.3125 to 0.3125
Outputs:
- input_grad: float32 [2, 16, 128, 32, 128], P('ex', None, 'slab')
- kernel_grad: float32 [2, 32, 432], replicated
The draws below stay inside these ranges and needn't reach their ends.
All inputs are finite; a program needn't handle non-finite values. No bound on the sum of `gate_mask` on one device may be relied on, other than what follows from the above.
Results may differ from the reference program's by a relative error of at most 0.0037.
Values may be sent and summed in bfloat16 or wider, within the bound.
A program may use at most 64 MiB of HBM per device.

```python
import math
import jax
import jax.numpy as jnp
from jax import lax

C = 16
DEPTH = 128
H = 32
W = 128
EX = 2


def draw_cotangent(key, part):
    key_base = jax.random.fold_in(key, 11)
    key_chan = jax.random.fold_in(key, 12)
    base = jax.random.normal(key_base, (EX, C, DEPTH, H, W), jnp.float32)
    base = jnp.clip(base, -4.0, 4.0)
    chan_scale = jnp.exp(jax.random.uniform(key_chan, (EX, C, 1, 1, 1), jnp.float32, jnp.log(0.5), jnp.log(5.0)))
    return (base * chan_scale * 0.3).astype(jnp.bfloat16)


def place_ends(result, rng, smallest, top_value):
    longest = result.shape.index(max(result.shape))
    spots = []
    for shift in (0, 1):
        where = [jax.random.randint(jax.random.fold_in(rng, axis), (), 0, length) for axis, length in enumerate(result.shape)]
        where[longest] = (where[longest] + shift) % result.shape[longest]
        spots.append(tuple(where))
    return result.at[spots[0]].set(smallest).at[spots[1]].set(top_value)


def block_levels(rng, extent, split, low, largest):
    loudness, own = 1.0, jax.random.fold_in(rng, 6)
    for dim, parts in split:
        steps = jnp.exp(jax.random.uniform(jax.random.fold_in(own, dim), (parts,), jnp.float32, low / len(split), largest / len(split)))
        loudness = loudness * jnp.repeat(steps, extent[dim] // parts).reshape([-1 if axis == dim else 1 for axis in range(len(extent))])
    return loudness


def normal_values(own_key, dims, spread, reach, shards=(), kind=jnp.bfloat16):
    values = jax.random.normal(own_key, dims, jnp.float32) * spread
    if len(shards) > 0:
        values = block_levels(own_key, dims, shards, -0.22, 0.18) * values
    return jnp.clip(values, min=-reach, max=reach).astype(kind)


def setup_inputs(seed: int = 0) -> dict:
    seeds = jax.random.split(jax.random.key(seed), 7)
    volume = normal_values(seeds[0], (EX, C, DEPTH, H, W), 1.0, 6.0, ((0, 2), (2, 128)))
    cotangent = draw_cotangent(jax.random.fold_in(seeds[6], 71), 0)
    gate_mask = place_ends((jax.random.randint(seeds[2], (EX, 2, DEPTH, H, W), 0, 4) < 3).astype(jnp.int32), jax.random.fold_in(seeds[2], 1), 0, 1)
    loss_scale = jnp.clip(jnp.exp(math.log(5.0) - 4.6051702 * jax.random.uniform(seeds[3], (EX,), jnp.float32) ** block_levels(seeds[3], (EX,), ((0, 2),), -0.2, 0.2)), 0.05, 5.0)
    canary = jax.random.randint(seeds[4], (EX,), 0, C).astype(jnp.int32)
    kernels = normal_values(seeds[5], (2, 2 * C, 27 * C), (27 * C) ** -0.5, 0.3125)
    return dict(volume=volume, cotangent=cotangent, gate_mask=gate_mask, loss_scale=loss_scale, canary=canary, kernels=kernels)


def columns(field):
    zs, hs, ws = (field.shape[1], field.shape[2], field.shape[3])
    padded = jnp.pad(field, ((0, 0), (1, 1), (1, 1), (1, 1)))
    taps = []
    for dz in range(3):
        for dh in range(3):
            for dw in range(3):
                taps.append(padded[:, dz:dz + zs, dh:dh + hs, dw:dw + ws])
    stacked = jnp.stack(taps, axis=0)
    return stacked.reshape((27 * field.shape[0], zs, hs, ws))

def back_columns(field):
    zs, hs, ws = (field.shape[1], field.shape[2], field.shape[3])
    padded = jnp.pad(field, ((0, 0), (1, 1), (1, 1), (1, 1)))
    taps = []
    for dz in range(3):
        for dh in range(3):
            for dw in range(3):
                taps.append(padded[:, 2 - dz:2 - dz + zs, 2 - dh:2 - dh + hs, 2 - dw:2 - dw + ws])
    return jnp.stack(taps, axis=0)

def forward_conv(kernel, field):
    return jnp.einsum('ok,kzhw->ozhw', kernel.astype(jnp.float32), columns(field).astype(jnp.float32))

def transposed_conv(kernel, grads):
    shaped = kernel.astype(jnp.float32).reshape((2 * C, 27, C))
    return jnp.einsum('otc,tozhw->czhw', shaped, back_columns(grads).astype(jnp.float32))

def kernel_product(grads, field):
    return jnp.einsum('ozhw,kzhw->ok', grads.astype(jnp.float32), columns(field).astype(jnp.float32))

def one_example(volume, cotangent, gate_mask, loss_scale, canary, kernels):
    mask_one = gate_mask[0].astype(jnp.float32)
    mask_two = gate_mask[1].astype(jnp.float32)
    pre_one = forward_conv(kernels[0], volume)
    value_one = pre_one[:C]
    sig_one = jax.nn.sigmoid(pre_one[C:])
    hidden = (volume.astype(jnp.float32) + value_one * sig_one * mask_one).astype(jnp.bfloat16)
    pre_two = forward_conv(kernels[1], hidden)
    value_two = pre_two[:C]
    sig_two = jax.nn.sigmoid(pre_two[C:])
    weights = 1.0 + 2.0 * (jnp.arange(C, dtype=jnp.int32) == canary).astype(jnp.float32)
    grad_out = cotangent.astype(jnp.float32) * loss_scale * weights[:, None, None, None]
    delta_two = jnp.concatenate([grad_out * sig_two * mask_two, grad_out * value_two * sig_two * (1.0 - sig_two) * mask_two], axis=0).astype(jnp.bfloat16)
    grad_two = kernel_product(delta_two, hidden)
    grad_hidden = grad_out + transposed_conv(kernels[1], delta_two)
    delta_one = jnp.concatenate([grad_hidden * sig_one * mask_one, grad_hidden * value_one * sig_one * (1.0 - sig_one) * mask_one], axis=0).astype(jnp.bfloat16)
    grad_one = kernel_product(delta_one, volume)
    input_grad = grad_hidden + transposed_conv(kernels[0], delta_one)
    stacked = jnp.stack([grad_one, grad_two], axis=0)
    norm = jnp.sqrt(jnp.sum(stacked * stacked) + 1e-06)
    bound = 20.0 * jnp.sqrt(jnp.float32(DEPTH * H * W))
    factor = jnp.minimum(1.0, bound / norm)
    return (input_grad, stacked * factor)

def reference(volume, cotangent, gate_mask, loss_scale, canary, kernels):

    def single(items):
        return one_example(items[0], items[1], items[2], items[3], items[4], kernels)
    input_grad, clipped = lax.map(single, (volume, cotangent, gate_mask, loss_scale, canary))
    bound = 20.0 * jnp.sqrt(jnp.float32(DEPTH * H * W))
    scaling = jnp.sqrt(jnp.float32(108 * C * C)) / (bound * jnp.sqrt(jnp.float32(EX)))
    kernel_grad = lax.optimization_barrier(jnp.sum(clipped, axis=0)) * scaling
    return (input_grad, kernel_grad)
```

```python
import functools
import jax
import jax.numpy as jnp
from jax import lax
from jax.experimental import pallas as pl
from jax.experimental.pallas import tpu as pltpu
from jax.sharding import PartitionSpec as P

F32 = jnp.float32
BF16 = jnp.bfloat16
MESH = pl.DeviceIdType.MESH
C = 16
H = 32
W = 128
NC = 4
HC = H // NC
CW = HC * W
PW = (H + 2) * W


def torus_of(slabs):
    return {128: (4, 4, 8), 8: (2, 2, 2)}[slabs]


def kernel(torus, depth, vol, cot, mask, scale, canary, ker, dx_out, kg_out,
           tmp, xb, db, kbt, kb, mk, a1, b1, dy, own, bsend, brecv, gpad,
           gs, rsr, zr, ag, ps, pr,
           xs_sem, xr_sem, bs_sem, br_sem, rs_s, rs_r, z_s, z_r, ag_s, ag_r, p_s, p_r):
    nx, ny, nz = torus
    gxy = nx * ny
    slabs = gxy * nz
    me = lax.axis_index("slab")
    ex = lax.axis_index("ex")
    up = lax.rem(me + 1, slabs)
    down = lax.rem(me + slabs - 1, slabs)
    mz = me // gxy
    mxy = lax.rem(me, gxy)
    my = mxy // nx
    mx = lax.rem(mxy, nx)
    offs = [(a, b) for b in range(ny) for a in range(nx) if (a, b) != (0, 0)]
    offs.sort(key=lambda o: -(min(o[0], nx - o[0]) + min(o[1], ny - o[1])))
    zoffs = sorted(range(1, nz), key=lambda o: -min(o, nz - o))

    def xy_peer(o):
        return lax.rem(my + o[1], ny) * nx + lax.rem(mx + o[0], nx)

    barrier = pltpu.get_barrier_semaphore()
    for t in (up, down):
        pl.semaphore_signal(barrier, inc=1, device_id={"slab": t}, device_id_type=MESH)
    for o in offs:
        pl.semaphore_signal(barrier, inc=1, device_id={"slab": mz * gxy + xy_peer(o)}, device_id_type=MESH)
    for o in zoffs:
        pl.semaphore_signal(barrier, inc=1, device_id={"slab": lax.rem(mz + o, nz) * gxy + mxy}, device_id_type=MESH)
    pl.semaphore_signal(barrier, inc=1, device_id={"ex": 1 - ex}, device_id_type=MESH)

    lane = lax.broadcasted_iota(jnp.int32, (C, W), 1)
    first = lane == 0
    last = lane == W - 1
    has_down = me > 0
    has_up = me < slabs - 1

    def shifts(x):
        rows = x.shape[0] // C
        left, right = [], []
        for i in range(rows):
            part = x[i * C:(i + 1) * C, :].astype(F32)
            left.append(jnp.where(first, 0.0, pltpu.roll(part, 1, 1)).astype(BF16))
            right.append(jnp.where(last, 0.0, pltpu.roll(part, W - 1, 1)).astype(BF16))
        if rows == 1:
            return left[0], right[0]
        return jnp.concatenate(left, axis=0), jnp.concatenate(right, axis=0)

    def fill(layer, dz, k):
        for i in range(HC):
            at = pl.ds((1 + k * HC + i) * W, W)
            x = xb[layer, dz * 3 + 1, :, at]
            if dz != 1:
                x = jnp.where(has_down if dz == 0 else has_up, x.astype(F32), 0.0).astype(BF16)
                xb[layer, dz * 3 + 1, :, at] = x
            left, right = shifts(x)
            xb[layer, dz * 3, :, at] = left
            xb[layer, dz * 3 + 2, :, at] = right

    def cols(layer, k):
        parts = []
        for dz in range(3):
            for dh in range(3):
                for dw in range(3):
                    parts.append(xb[layer, dz * 3 + dw, :, pl.ds((k * HC + dh) * W, CW)])
        return jnp.concatenate(parts, axis=0)

    def back_cols(layer, k):
        parts = []
        for dh in range(3):
            for dw in range(3):
                parts.append(db[layer, dw, :, pl.ds((k * HC + 2 - dh) * W, CW)])
        return jnp.concatenate(parts, axis=0)

    def halo_copies(layer, k):
        at = pl.ds((1 + k * HC) * W, CW)
        src = xb.at[layer, 4, :, at]
        made = []
        for side, (dz, peer) in enumerate(((0, up), (2, down))):
            made.append(pltpu.make_async_remote_copy(
                src_ref=src, dst_ref=xb.at[layer, dz * 3 + 1, :, at],
                send_sem=xs_sem.at[layer, side, k], recv_sem=xr_sem.at[layer, side, k],
                device_id={"slab": peer}, device_id_type=MESH))
        return made

    def back_copies(layer, k):
        at = pl.ds(k * CW, CW)
        made = []
        for side, peer in enumerate((up, down)):
            made.append(pltpu.make_async_remote_copy(
                src_ref=bsend.at[layer, side, :, at], dst_ref=brecv.at[layer, side, :, at],
                send_sem=bs_sem.at[layer, side, k], recv_sem=br_sem.at[layer, side, k],
                device_id={"slab": peer}, device_id_type=MESH))
        return made

    def store_delta(layer, k, delta):
        for i in range(HC):
            at = pl.ds((1 + k * HC + i) * W, W)
            x = delta[:, i * W:(i + 1) * W]
            left, right = shifts(x)
            db[layer, 1, :, at] = x
            db[layer, 2, :, at] = left
            db[layer, 0, :, at] = right

    def back(layer, k):
        got = jnp.dot(kb[layer], back_cols(layer, k), preferred_element_type=F32)
        at = pl.ds(k * CW, CW)
        own[:, at] = got[C:2 * C]
        bsend[layer, 1, :, at] = got[:C].astype(BF16)
        bsend[layer, 0, :, at] = got[2 * C:].astype(BF16)

    def back_total(layer, k):
        at = pl.ds(k * CW, CW)
        below = jnp.where(has_down, brecv[layer, 0, :, at].astype(F32), 0.0)
        above = jnp.where(has_up, brecv[layer, 1, :, at].astype(F32), 0.0)
        return own[:, at] + below + above

    def weight_grad(layer, k):
        d = db[layer, 1, :, pl.ds((1 + k * HC) * W, CW)]
        return lax.dot_general(d, cols(layer, k), (((1,), (1,)), ((), ())), preferred_element_type=F32)

    tmp[...] = vol[...].astype(F32)
    for h in range(H):
        xb[0, 4, :, pl.ds((1 + h) * W, W)] = tmp[:, h, :].astype(BF16)
    zero_row = jnp.zeros((C, W), BF16)
    for edge in (0, H + 1):
        at = pl.ds(edge * W, W)
        for layer in range(2):
            for q in range(9):
                xb[layer, q, :, at] = zero_row
            for q in range(3):
                db[layer, q, :C, at] = zero_row
                db[layer, q, C:, at] = zero_row
    gpad[...] = jnp.zeros_like(gpad)
    pl.semaphore_wait(barrier, 2 + len(offs) + len(zoffs) + 1)

    for k in range(NC):
        for copy in halo_copies(0, k):
            copy.start()

    for k in range(NC):
        fill(0, 1, k)
    for h in range(H):
        for q in range(2):
            row = mask[q, h:h + 1, :].astype(F32)
            mk[q, :, pl.ds(h * W, W)] = jnp.broadcast_to(row, (C, W))
    for layer in range(2):
        kf = ker[layer].astype(F32)
        for dh in range(3):
            for dw in range(3):
                for dz in range(3):
                    t = 9 * dz + 3 * dh + dw
                    kbt[pl.ds((dh * 3 + dw) * 2 * C, 2 * C), dz * C:(dz + 1) * C] = kf[:, t * C:(t + 1) * C]
        kb[layer] = jnp.transpose(kbt[...])[:3 * C].astype(BF16)
    tmp[...] = cot[...].astype(F32)
    chan = lax.broadcasted_iota(jnp.int32, (C, W), 0)
    weight = jnp.where(chan == canary[0], 3.0, 1.0).astype(F32)
    for h in range(H):
        dy[:, pl.ds(h * W, W)] = tmp[:, h, :] * scale[0] * weight

    def layer_one(k):
        pre = jnp.dot(ker[0], cols(0, k), preferred_element_type=F32)
        at = pl.ds(k * CW, CW)
        pat = pl.ds((1 + k * HC) * W, CW)
        v = pre[:C]
        s = jax.nn.sigmoid(pre[C:])
        sm = s * mk[0, :, at]
        a1[:, at] = sm
        b1[:, at] = v * sm * (1.0 - s)
        xb[1, 4, :, pat] = (xb[0, 4, :, pat].astype(F32) + v * sm).astype(BF16)
        for copy in halo_copies(1, k):
            copy.start()
        fill(1, 1, k)

    for k in range(NC):
        for copy in halo_copies(0, k):
            copy.wait_recv()
        fill(0, 0, k)
        fill(0, 2, k)
        if k > 0:
            layer_one(k - 1)
    layer_one(NC - 1)

    def layer_two(k):
        pre = jnp.dot(ker[1], cols(1, k), preferred_element_type=F32)
        at = pl.ds(k * CW, CW)
        v = pre[:C]
        s = jax.nn.sigmoid(pre[C:])
        g = dy[:, at] * (s * mk[1, :, at])
        delta = jnp.concatenate([g, g * v * (1.0 - s)], axis=0).astype(BF16)
        store_delta(1, k, delta)

    def back_send(layer, k):
        back(layer, k)
        for copy in back_copies(layer, k):
            copy.start()

    for k in range(NC):
        for copy in halo_copies(1, k):
            copy.wait_recv()
        fill(1, 0, k)
        fill(1, 2, k)
        if k > 0:
            layer_two(k - 1)
        if k > 1:
            back_send(1, k - 2)
    layer_two(NC - 1)
    back_send(1, NC - 2)
    back_send(1, NC - 1)

    g2 = weight_grad(1, 0)
    for k in range(1, NC):
        g2 = g2 + weight_grad(1, k)
    gpad[1, :, :27 * C] = g2

    g1 = None
    for k in range(NC):
        at = pl.ds(k * CW, CW)
        for copy in back_copies(1, k):
            copy.wait_recv()
        dx = dy[:, at] + back_total(1, k)
        dy[:, at] = dx
        delta = jnp.concatenate([dx * a1[:, at], dx * b1[:, at]], axis=0).astype(BF16)
        store_delta(0, k, delta)
        part = weight_grad(0, k)
        g1 = part if k == 0 else g1 + part
    gpad[0, :, :27 * C] = g1

    tiles = 16 // gxy
    for j in range(16):
        i, n = j // 4, j % 4
        for layer in range(2):
            gs[j // tiles, layer, j % tiles] = gpad[layer, i * 8:(i + 1) * 8, n * W:(n + 1) * W]

    def rs_copy(o):
        r = o[1] * nx + o[0]
        peer = xy_peer(o)
        return pltpu.make_async_remote_copy(
            src_ref=gs.at[peer], dst_ref=rsr.at[r], send_sem=rs_s.at[r], recv_sem=rs_r.at[r],
            device_id={"slab": mz * gxy + peer}, device_id_type=MESH)

    def z_copy(o):
        return pltpu.make_async_remote_copy(
            src_ref=zr.at[mz], dst_ref=zr.at[mz], send_sem=z_s.at[o], recv_sem=z_r.at[o],
            device_id={"slab": lax.rem(mz + o, nz) * gxy + mxy}, device_id_type=MESH)

    def ag_copy(o):
        r = o[1] * nx + o[0]
        return pltpu.make_async_remote_copy(
            src_ref=ag.at[mxy], dst_ref=ag.at[mxy], send_sem=ag_s.at[r], recv_sem=ag_r.at[r],
            device_id={"slab": mz * gxy + xy_peer(o)}, device_id_type=MESH)

    for o in offs:
        rs_copy(o).start()
    for k in range(NC):
        back_send(0, k)
    for o in offs:
        rs_copy(o).wait_recv()
    total = gs[mxy]
    for o in offs:
        total = total + rsr[o[1] * nx + o[0]]
    zr[mz] = total
    for o in zoffs:
        z_copy(o).start()

    for k in range(NC):
        for copy in back_copies(0, k):
            copy.wait_recv()
        at = pl.ds(k * CW, CW)
        res = dy[:, at] + back_total(0, k)
        for i in range(HC):
            dx_out[:, k * HC + i, :] = res[:, i * W:(i + 1) * W]

    for o in zoffs:
        z_copy(o).wait()
    total = zr[0]
    for q in range(1, nz):
        total = total + zr[q]
    ag[mxy] = total
    for o in offs:
        ag_copy(o).start()
    for o in offs:
        ag_copy(o).wait()

    bound = 20.0 * float(depth * H * W) ** 0.5
    square = None
    for q in range(gxy):
        for layer in range(2):
            for t in range(tiles):
                x = ag[q, layer, t]
                square = x * x if square is None else square + x * x
    norm = jnp.sqrt(jnp.sum(square, keepdims=True) + 1e-06)
    scaling = float(108 * C * C) ** 0.5 / (bound * 2.0 ** 0.5)
    factor = jnp.minimum(1.0, bound / norm)
    for q in range(gxy):
        for layer in range(2):
            for t in range(tiles):
                ps[q, layer, t] = ag[q, layer, t] * factor
    swap = pltpu.make_async_remote_copy(
        src_ref=ps, dst_ref=pr, send_sem=p_s, recv_sem=p_r,
        device_id={"ex": 1 - ex}, device_id_type=MESH)
    swap.start()
    swap.wait()
    for j in range(16):
        i, n = j // 4, j % 4
        width = min(W, 27 * C - n * W)
        for layer in range(2):
            x = (ps[j // tiles, layer, j % tiles] + pr[j // tiles, layer, j % tiles]) * scaling
            kg_out[layer, i * 8:(i + 1) * 8, n * W:n * W + width] = x[:, :width]

    for k in range(NC):
        for layer in range(2):
            for copy in halo_copies(layer, k):
                copy.wait_send()
            for copy in back_copies(layer, k):
                copy.wait_send()
    for o in offs:
        rs_copy(o).wait_send()


def per_device(volume, cotangent, gate_mask, loss_scale, canary, kernels):
    slabs = lax.axis_size("slab")
    torus = torus_of(slabs)
    nx, ny, nz = torus
    gxy = nx * ny
    tiles = 16 // gxy
    vm = pl.BlockSpec(memory_space=pltpu.VMEM)
    sm = pl.BlockSpec(memory_space=pltpu.SMEM)
    dma = pltpu.SemaphoreType.DMA
    part = (2, tiles, 8, W)
    dx, kg = pl.pallas_call(
        functools.partial(kernel, torus, slabs),
        out_shape=(jax.ShapeDtypeStruct((C, H, W), F32), jax.ShapeDtypeStruct((2, 2 * C, 27 * C), F32)),
        in_specs=[vm, vm, vm, sm, sm, vm],
        out_specs=(vm, vm),
        scratch_shapes=[
            pltpu.VMEM((C, H, W), F32),
            pltpu.VMEM((2, 9, C, PW), BF16),
            pltpu.VMEM((2, 3, 2 * C, PW), BF16),
            pltpu.VMEM((18 * C, W), F32),
            pltpu.VMEM((2, 3 * C, 18 * C), BF16),
            pltpu.VMEM((2, C, H * W), F32),
            pltpu.VMEM((C, H * W), F32),
            pltpu.VMEM((C, H * W), F32),
            pltpu.VMEM((C, H * W), F32),
            pltpu.VMEM((C, H * W), F32),
            pltpu.VMEM((2, 2, C, H * W), BF16),
            pltpu.VMEM((2, 2, C, H * W), BF16),
            pltpu.VMEM((2, 2 * C, 4 * W), F32),
            pltpu.VMEM((gxy,) + part, F32),
            pltpu.VMEM((gxy,) + part, F32),
            pltpu.VMEM((nz,) + part, F32),
            pltpu.VMEM((gxy,) + part, F32),
            pltpu.VMEM((gxy,) + part, F32),
            pltpu.VMEM((gxy,) + part, F32),
            dma((2, 2, NC)), dma((2, 2, NC)), dma((2, 2, NC)), dma((2, 2, NC)),
            dma((gxy,)), dma((gxy,)), dma((nz,)), dma((nz,)), dma((gxy,)), dma((gxy,)),
            dma, dma,
        ],
        compiler_params=pltpu.CompilerParams(
            collective_id=0, has_side_effects=True, vmem_limit_bytes=48 * 1024 * 1024),
        name="gated_level",
    )(
        volume.reshape((C, H, W)),
        cotangent.reshape((C, H, W)),
        gate_mask.reshape((2, H, W)),
        loss_scale,
        canary,
        kernels,
    )
    return dx.reshape((1, C, 1, H, W)), kg


def solution(mesh):
    placed = (
        P("ex", None, "slab", None, None),
        P("ex", None, "slab", None, None),
        P("ex", None, "slab", None, None),
        P("ex"),
        P("ex"),
        P(),
    )
    return jax.shard_map(
        per_device,
        mesh=mesh,
        in_specs=placed,
        out_specs=(P("ex", None, "slab", None, None), P()),
        check_vma=False,
    )
```

```python
import functools
import jax
import jax.numpy as jnp
from jax import lax
from jax.experimental import pallas as pl
from jax.experimental.pallas import tpu as pltpu
from jax.sharding import PartitionSpec as P

F32 = jnp.float32
BF16 = jnp.bfloat16
MESH = pl.DeviceIdType.MESH
C = 16
H = 32
W = 128
PW = (H + 2) * W
ROWS = (
    (0, 10, 20, 28, 32),
    (0, 9, 19, 27, 32),
    (0, 8, 18, 26, 32),
    (0, 7, 17, 25, 32),
)
NC = len(ROWS[0]) - 1


def torus_of(slabs):
    return {128: (4, 4, 8), 8: (2, 2, 2)}[slabs]


def spans(stage, k):
    return ROWS[stage][k], ROWS[stage][k + 1]


def flat(r0, r1):
    return pl.ds(r0 * W, (r1 - r0) * W)


def kernel(torus, depth, vol_hbm, cot_hbm, mask_hbm, scale, canary, ker_hbm, dx_out, kg_out,
           vol, cot, mask, ker, tmp, xb, db, kbt, kb, mk, a1, b1, dy, own, bsend, brecv, gpad,
           gs, rsr, zr, ag, kgs,
           xs_sem, xr_sem, bs_sem, br_sem, rs_s, rs_r, z_s, z_r, ag_s, ag_r, p_s, p_r, in_sem):
    nx, ny, nz = torus
    gxy = nx * ny
    slabs = gxy * nz
    me = lax.axis_index("slab")
    ex = lax.axis_index("ex")
    mz = me // gxy
    mxy = lax.rem(me, gxy)
    my = mxy // nx
    mx = lax.rem(mxy, nx)
    offs = [(a, b) for b in range(ny) for a in range(nx) if (a, b) != (0, 0)]
    offs.sort(key=lambda o: -(min(o[0], nx - o[0]) + min(o[1], ny - o[1])))
    zoffs = sorted(range(1, nz), key=lambda o: -min(o, nz - o))
    tiles = 16 // gxy
    slots = ((1, 1), (1, 0), (0, 1), (0, 0))
    groups = ((0, 3), (3, 1))
    has_down = me > 0
    has_up = me < slabs - 1
    up = jnp.minimum(me + 1, slabs - 1)
    down = jnp.maximum(me - 1, 0)

    def xy_peer(o):
        return lax.rem(my + o[1], ny) * nx + lax.rem(mx + o[0], nx)

    def signal(device):
        pl.semaphore_signal(barrier, inc=1, device_id=device, device_id_type=MESH)

    barrier = pltpu.get_barrier_semaphore()

    @pl.when(has_up)
    def _():
        signal({"slab": up})

    @pl.when(has_down)
    def _():
        signal({"slab": down})

    @pl.when(ex == 1)
    def _():
        for o in offs:
            for e in range(2):
                signal({"ex": e, "slab": mz * gxy + xy_peer(o)})
        for o in zoffs:
            signal({"slab": lax.rem(mz + o, nz) * gxy + mxy})

    signal({"ex": 1 - ex})
    loads = [pltpu.make_async_copy(src, dst, in_sem.at[q]) for q, (src, dst) in enumerate(
        ((vol_hbm, vol), (ker_hbm, ker), (mask_hbm, mask), (cot_hbm, cot)))]
    for load in loads:
        load.start()
    lane = lax.broadcasted_iota(jnp.int32, (C, W), 1)
    first = lane == 0
    last = lane == W - 1

    def shifts(x):
        rows = x.shape[0] // C
        left, right = [], []
        for i in range(rows):
            part = x[i * C:(i + 1) * C, :].astype(F32)
            left.append(jnp.where(first, 0.0, pltpu.roll(part, 1, 1)).astype(BF16))
            right.append(jnp.where(last, 0.0, pltpu.roll(part, W - 1, 1)).astype(BF16))
        if rows == 1:
            return left[0], right[0]
        return jnp.concatenate(left, axis=0), jnp.concatenate(right, axis=0)

    def fill(layer, dz, rows):
        for r in range(*rows):
            at = flat(1 + r, 2 + r)
            x = xb[layer, dz * 3 + 1, :, at]
            if dz != 1:
                x = jnp.where(has_down if dz == 0 else has_up, x.astype(F32), 0.0).astype(BF16)
                xb[layer, dz * 3 + 1, :, at] = x
            left, right = shifts(x)
            xb[layer, dz * 3, :, at] = left
            xb[layer, dz * 3 + 2, :, at] = right

    def cols(layer, rows):
        parts = []
        for dz in range(3):
            for dh in range(3):
                for dw in range(3):
                    parts.append(xb[layer, dz * 3 + dw, :, flat(rows[0] + dh, rows[1] + dh)])
        return jnp.concatenate(parts, axis=0)

    def back_cols(layer, rows):
        parts = []
        for dh in range(3):
            for dw in range(3):
                parts.append(db[layer, dw, :, flat(rows[0] + 2 - dh, rows[1] + 2 - dh)])
        return jnp.concatenate(parts, axis=0)

    def halo_copy(layer, side, k):
        r0, r1 = spans(layer, k)
        at = flat(1 + r0, 1 + r1)
        return pltpu.make_async_remote_copy(
            src_ref=xb.at[layer, 4, :, at], dst_ref=xb.at[layer, 6 * side + 1, :, at],
            send_sem=xs_sem.at[layer, side, k], recv_sem=xr_sem.at[layer, side, k],
            device_id={"slab": (up, down)[side]}, device_id_type=MESH)

    def back_copy(layer, side, k):
        at = flat(*spans(3, k))
        return pltpu.make_async_remote_copy(
            src_ref=bsend.at[layer, side, :, at], dst_ref=brecv.at[layer, side, :, at],
            send_sem=bs_sem.at[layer, side, k], recv_sem=br_sem.at[layer, side, k],
            device_id={"slab": (up, down)[side]}, device_id_type=MESH)

    def start(copy, layer, k):
        @pl.when(has_up)
        def _():
            copy(layer, 0, k).start()

        @pl.when(has_down)
        def _():
            copy(layer, 1, k).start()

    def arrive(copy, layer, k):
        @pl.when(has_down)
        def _():
            copy(layer, 0, k).wait_recv()

        @pl.when(has_up)
        def _():
            copy(layer, 1, k).wait_recv()

    def sent(copy, layer):
        @pl.when(has_up)
        def _():
            for k in range(NC):
                copy(layer, 0, k).wait_send()

        @pl.when(has_down)
        def _():
            for k in range(NC):
                copy(layer, 1, k).wait_send()

    def store_delta(layer, rows, delta):
        for i, r in enumerate(range(*rows)):
            at = flat(1 + r, 2 + r)
            x = delta[:, i * W:(i + 1) * W]
            left, right = shifts(x)
            db[layer, 1, :, at] = x
            db[layer, 2, :, at] = left
            db[layer, 0, :, at] = right

    def back(layer, rows):
        got = jnp.dot(kb[layer], back_cols(layer, rows), preferred_element_type=F32)
        at = flat(*rows)
        own[:, at] = got[C:2 * C]
        bsend[layer, 1, :, at] = got[:C].astype(BF16)
        bsend[layer, 0, :, at] = got[2 * C:].astype(BF16)

    def back_total(layer, rows):
        at = flat(*rows)
        below = jnp.where(has_down, brecv[layer, 0, :, at].astype(F32), 0.0)
        above = jnp.where(has_up, brecv[layer, 1, :, at].astype(F32), 0.0)
        return own[:, at] + below + above

    def weight_grad(layer, rows):
        d = db[layer, 1, :, flat(1 + rows[0], 1 + rows[1])]
        return lax.dot_general(d, cols(layer, rows), (((1,), (1,)), ((), ())), preferred_element_type=F32)

    loads[0].wait()
    tmp[...] = vol[...].astype(F32)
    for h in range(H):
        xb[0, 4, :, flat(1 + h, 2 + h)] = tmp[:, h, :].astype(BF16)
    zero_row = jnp.zeros((C, W), BF16)
    for edge in (0, H + 1):
        at = flat(edge, edge + 1)
        for layer in range(2):
            for q in range(9):
                xb[layer, q, :, at] = zero_row
            for q in range(3):
                db[layer, q, :C, at] = zero_row
                db[layer, q, C:, at] = zero_row
    gpad[...] = jnp.zeros_like(gpad)
    many = jnp.where(ex == 1, len(offs) + len(zoffs) + 1, len(offs) + 1)
    pl.semaphore_wait(barrier, many + has_up.astype(jnp.int32) + has_down.astype(jnp.int32))
    for k in range(NC):
        start(halo_copy, 0, k)
    fill(0, 1, (0, H))
    for load in loads[1:]:
        load.wait()
    for h in range(H):
        for q in range(2):
            row = mask[q, h:h + 1, :].astype(F32)
            mk[q, :, flat(h, h + 1)] = jnp.broadcast_to(row, (C, W))
    for layer in range(2):
        kf = ker[layer].astype(F32)
        for dh in range(3):
            for dw in range(3):
                for dz in range(3):
                    t = 9 * dz + 3 * dh + dw
                    kbt[pl.ds((dh * 3 + dw) * 2 * C, 2 * C), dz * C:(dz + 1) * C] = kf[:, t * C:(t + 1) * C]
        kb[layer] = jnp.transpose(kbt[...])[:3 * C].astype(BF16)
    tmp[...] = cot[...].astype(F32)
    chan = lax.broadcasted_iota(jnp.int32, (C, W), 0)
    weight = jnp.where(chan == canary[0], 3.0, 1.0).astype(F32)
    for h in range(H):
        dy[:, flat(h, h + 1)] = tmp[:, h, :] * scale[0] * weight

    def layer_one(rows):
        pre = jnp.dot(ker[0], cols(0, rows), preferred_element_type=F32)
        at = flat(*rows)
        pat = flat(1 + rows[0], 1 + rows[1])
        v = pre[:C]
        s = jax.nn.sigmoid(pre[C:])
        sm = s * mk[0, :, at]
        a1[:, at] = sm
        b1[:, at] = v * sm * (1.0 - s)
        xb[1, 4, :, pat] = (xb[0, 4, :, pat].astype(F32) + v * sm).astype(BF16)

    def layer_two(rows):
        pre = jnp.dot(ker[1], cols(1, rows), preferred_element_type=F32)
        at = flat(*rows)
        v = pre[:C]
        s = jax.nn.sigmoid(pre[C:])
        g = dy[:, at] * (s * mk[1, :, at])
        delta = jnp.concatenate([g, g * v * (1.0 - s)], axis=0).astype(BF16)
        store_delta(1, rows, delta)

    def spread(layer, g):
        gpad[layer, :, :27 * C] = g
        for j in range(16):
            i, n = j // 4, j % 4
            gs[layer, j // tiles, j % tiles] = gpad[layer, i * 8:(i + 1) * 8, n * W:(n + 1) * W]

    def rs_copy(layer, o, e):
        r = o[1] * nx + o[0]
        peer = xy_peer(o)
        return pltpu.make_async_remote_copy(
            src_ref=gs.at[layer, peer], dst_ref=rsr.at[e, layer, r],
            send_sem=rs_s.at[layer, r], recv_sem=rs_r.at[e, layer, r],
            device_id={"ex": 1, "slab": mz * gxy + peer}, device_id_type=MESH)

    def rs_start(layer):
        for o in offs:
            rs_copy(layer, o, ex).start()

        @pl.when(ex == 0)
        def _():
            rs_copy(layer, (0, 0), 0).start()

    def z_copy(group, o):
        at = pl.ds(*groups[group])
        return pltpu.make_async_remote_copy(
            src_ref=zr.at[mz, at], dst_ref=zr.at[mz, at],
            send_sem=z_s.at[group, o], recv_sem=z_r.at[group, o],
            device_id={"slab": lax.rem(mz + o, nz) * gxy + mxy}, device_id_type=MESH)

    def ag_copy(group, o):
        r = o[1] * nx + o[0]
        at = pl.ds(*groups[group])
        return pltpu.make_async_remote_copy(
            src_ref=ag.at[mxy, at], dst_ref=ag.at[mxy, at],
            send_sem=ag_s.at[group, r], recv_sem=ag_r.at[group, r],
            device_id={"slab": mz * gxy + xy_peer(o)}, device_id_type=MESH)

    hand = pltpu.make_async_remote_copy(
        src_ref=kgs, dst_ref=kgs, send_sem=p_s, recv_sem=p_r,
        device_id={"ex": 1 - ex}, device_id_type=MESH)

    def rs_total(group):
        first_slot, count = groups[group]
        for q in range(first_slot, first_slot + count):
            e, layer = slots[q]
            sources = offs if e == 1 else offs + [(0, 0)]
            for o in sources:
                rs_copy(layer, o, e).wait_recv()
            parts = [rsr[e, layer, o[1] * nx + o[0]] for o in sources]
            if e == 1:
                parts.append(gs[layer, mxy])
            while len(parts) > 1:
                parts = [a + b for a, b in zip(parts[::2], parts[1::2])]
            zr[mz, q] = parts[0]
        for o in zoffs:
            z_copy(group, o).start()

    def z_total(group):
        first_slot, count = groups[group]
        for o in zoffs:
            z_copy(group, o).wait_recv()
        for q in range(first_slot, first_slot + count):
            parts = [zr[i, q] for i in range(nz)]
            while len(parts) > 1:
                parts = [a + b for a, b in zip(parts[::2], parts[1::2])]
            ag[mxy, q] = parts[0]
        for o in offs:
            ag_copy(group, o).start()

    def input_grad():
        for k in range(NC):
            arrive(back_copy, 0, k)
        for r in range(0, H, 8):
            rows = (r, r + 8)
            res = dy[:, flat(*rows)] + back_total(0, rows)
            for i in range(8):
                dx_out[:, r + i, :] = res[:, i * W:(i + 1) * W]

    for k in range(NC):
        arrive(halo_copy, 0, k)
        fill(0, 0, spans(0, k))
        fill(0, 2, spans(0, k))
        layer_one(spans(1, k))
        start(halo_copy, 1, k)
        fill(1, 1, spans(1, k))
    for k in range(NC):
        arrive(halo_copy, 1, k)
        fill(1, 0, spans(1, k))
        fill(1, 2, spans(1, k))
        layer_two(spans(2, k))
        back(1, spans(3, k))
        start(back_copy, 1, k)
    spread(1, weight_grad(1, (0, 16)) + weight_grad(1, (16, H)))
    g1 = None
    for k in range(NC):
        rows = spans(3, k)
        at = flat(*rows)
        arrive(back_copy, 1, k)
        if k == NC - 1:
            rs_start(1)
        dx = dy[:, at] + back_total(1, rows)
        dy[:, at] = dx
        delta = jnp.concatenate([dx * a1[:, at], dx * b1[:, at]], axis=0).astype(BF16)
        store_delta(0, rows, delta)
        if k == 1:
            g1 = weight_grad(0, (0, rows[1]))
        elif k > 1:
            g1 = g1 + weight_grad(0, rows)
    spread(0, g1)
    rs_start(0)
    for r in range(0, H, 16):
        back(0, (r, r + 16))
    for k in range(NC):
        start(back_copy, 0, k)
    bound = 20.0 * float(depth * H * W) ** 0.5
    scaling = float(108 * C * C) ** 0.5 / (bound * 2.0 ** 0.5)

    def factor(e):
        square = None
        for q in range(4):
            if slots[q][0] == e:
                for j in range(16):
                    x = ag[j // tiles, q, j % tiles]
                    square = x * x if square is None else square + x * x
        norm = jnp.sqrt(jnp.sum(square, keepdims=True) + 1e-06)
        return jnp.minimum(1.0, bound / norm)

    @pl.when(ex == 1)
    def _():
        for group in range(2):
            rs_total(group)
        for group in range(2):
            z_total(group)
        input_grad()
        for group in range(2):
            for o in offs:
                ag_copy(group, o).wait_recv()
        factors = factor(0), factor(1)
        for layer in range(2):
            for j in range(16):
                i, n = j // 4, j % 4
                width = min(W, 27 * C - n * W)
                zero, one = ag[j // tiles, 3 - layer, j % tiles], ag[j // tiles, 1 - layer, j % tiles]
                both = (zero * factors[0] + one * factors[1]) * scaling
                kgs[layer, i * 8:(i + 1) * 8, n * W:n * W + width] = both[:, :width]
        hand.start()
        kg_out[...] = kgs[...]
        for group in range(2):
            for o in zoffs:
                z_copy(group, o).wait_send()
            for o in offs:
                ag_copy(group, o).wait_send()
        hand.wait_send()

    @pl.when(ex == 0)
    def _():
        input_grad()
        for layer in range(2):
            rs_copy(layer, (0, 0), 0).wait_send()
        hand.wait_recv()
        kg_out[...] = kgs[...]

    for layer in range(2):
        for o in offs:
            rs_copy(layer, o, ex).wait_send()
        sent(halo_copy, layer)
        sent(back_copy, layer)


def leave(dx_in, kg_in, dx_out, kg_out, sem):
    copies = [pltpu.make_async_copy(a, b, sem.at[i]) for i, (a, b) in enumerate(((dx_in, dx_out), (kg_in, kg_out)))]
    for copy in copies:
        copy.start()
    for copy in copies:
        copy.wait()


def in_hbm(x):
    return pltpu.with_memory_space_constraint(x, pltpu.HBM)


def per_device(volume, cotangent, gate_mask, loss_scale, canary, kernels):
    slabs = lax.axis_size("slab")
    torus = torus_of(slabs)
    nx, ny, nz = torus
    gxy = nx * ny
    part = (16 // gxy, 8, W)
    vm = pl.BlockSpec(memory_space=pltpu.VMEM)
    sm = pl.BlockSpec(memory_space=pltpu.SMEM)
    hbm = pl.BlockSpec(memory_space=pltpu.HBM)
    dma = pltpu.SemaphoreType.DMA
    shapes = (jax.ShapeDtypeStruct((C, H, W), F32), jax.ShapeDtypeStruct((2, 2 * C, 27 * C), F32))
    dx, kg = pl.pallas_call(
        functools.partial(kernel, torus, slabs),
        out_shape=shapes,
        in_specs=[hbm, hbm, hbm, sm, sm, hbm],
        out_specs=(vm, vm),
        scratch_shapes=[
            pltpu.VMEM((C, H, W), BF16),
            pltpu.VMEM((C, H, W), BF16),
            pltpu.VMEM((2, H, W), jnp.int32),
            pltpu.VMEM((2, 2 * C, 27 * C), BF16),
            pltpu.VMEM((C, H, W), F32),
            pltpu.VMEM((2, 9, C, PW), BF16),
            pltpu.VMEM((2, 3, 2 * C, PW), BF16),
            pltpu.VMEM((18 * C, W), F32),
            pltpu.VMEM((2, 3 * C, 18 * C), BF16),
            pltpu.VMEM((2, C, H * W), F32),
            pltpu.VMEM((C, H * W), F32),
            pltpu.VMEM((C, H * W), F32),
            pltpu.VMEM((C, H * W), F32),
            pltpu.VMEM((C, H * W), F32),
            pltpu.VMEM((2, 2, C, H * W), BF16),
            pltpu.VMEM((2, 2, C, H * W), BF16),
            pltpu.VMEM((2, 2 * C, 4 * W), F32),
            pltpu.VMEM((2, gxy) + part, F32),
            pltpu.VMEM((2, 2, gxy) + part, F32),
            pltpu.VMEM((nz, 4) + part, F32),
            pltpu.VMEM((gxy, 4) + part, F32),
            pltpu.VMEM((2, 2 * C, 27 * C), F32),
            dma((2, 2, NC)), dma((2, 2, NC)), dma((2, 2, NC)), dma((2, 2, NC)),
            dma((2, gxy)), dma((2, 2, gxy)), dma((2, nz)), dma((2, nz)), dma((2, gxy)), dma((2, gxy)),
            dma, dma, dma((4,)),
        ],
        compiler_params=pltpu.CompilerParams(
            collective_id=0, has_side_effects=True, vmem_limit_bytes=48 * 1024 * 1024),
        name="gated_level",
    )(
        in_hbm(volume.reshape((C, H, W))),
        in_hbm(cotangent.reshape((C, H, W))),
        in_hbm(gate_mask.reshape((2, H, W))),
        loss_scale,
        canary,
        in_hbm(kernels),
    )
    dx, kg = pl.pallas_call(
        leave,
        out_shape=shapes,
        in_specs=[vm, vm],
        out_specs=(hbm, hbm),
        scratch_shapes=[dma((2,))],
        compiler_params=pltpu.CompilerParams(vmem_limit_bytes=1024 * 1024),
        name="leave",
    )(dx, kg)
    return dx.reshape((1, C, 1, H, W)), kg


def solution(mesh):
    placed = (
        P("ex", None, "slab", None, None),
        P("ex", None, "slab", None, None),
        P("ex", None, "slab", None, None),
        P("ex"),
        P("ex"),
        P(),
    )
    return jax.shard_map(
        per_device,
        mesh=mesh,
        in_specs=placed,
        out_specs=(P("ex", None, "slab", None, None), P()),
        check_vma=False,
    )
```

```python
import functools
import jax
import jax.numpy as jnp
from jax import lax
from jax.experimental import pallas as pl
from jax.experimental.pallas import tpu as pltpu
from jax.sharding import PartitionSpec as P

F32 = jnp.float32
BF16 = jnp.bfloat16
MESH = pl.DeviceIdType.MESH
C = 16
H = 32
W = 128
PW = (H + 2) * W
ROWS = (
    (0, 10, 20, 28, 32),
    (0, 9, 19, 27, 32),
    (0, 8, 18, 26, 32),
    (0, 7, 17, 25, 32),
)
NC = len(ROWS[0]) - 1


def torus_of(slabs):
    return {128: (4, 4, 8), 8: (2, 2, 2)}[slabs]


def spans(stage, k):
    return ROWS[stage][k], ROWS[stage][k + 1]


def flat(r0, r1):
    return pl.ds(r0 * W, (r1 - r0) * W)


def kernel(torus, depth, vol_hbm, cot_hbm, mask_hbm, scale, canary, ker_hbm, dx_out, kg_out,
           vol, cot, mask, ker, tmp, xb, db, kbt, kb, mk, a1, b1, dy, own, bsend, brecv, gpad,
           gs, rsr, zr, ag, kgs,
           xs_sem, xr_sem, bs_sem, br_sem, rs_s, rs_r, z_s, z_r, ag_s, ag_r, p_s, p_r, in_sem):
    nx, ny, nz = torus
    gxy = nx * ny
    slabs = gxy * nz
    me = lax.axis_index("slab")
    ex = lax.axis_index("ex")
    mz = me // gxy
    mxy = lax.rem(me, gxy)
    my = mxy // nx
    mx = lax.rem(mxy, nx)
    offs = [(a, b) for b in range(ny) for a in range(nx) if (a, b) != (0, 0)]
    offs.sort(key=lambda o: -(min(o[0], nx - o[0]) + min(o[1], ny - o[1])))
    zoffs = sorted(range(1, nz), key=lambda o: -min(o, nz - o))
    tiles = 16 // gxy
    slots = ((1, 1), (1, 0), (0, 1), (0, 0))
    groups = ((0, 3), (3, 1))
    has_down = me > 0
    has_up = me < slabs - 1
    up = jnp.minimum(me + 1, slabs - 1)
    down = jnp.maximum(me - 1, 0)

    def xy_peer(o):
        return lax.rem(my + o[1], ny) * nx + lax.rem(mx + o[0], nx)

    def signal(device):
        pl.semaphore_signal(barrier, inc=1, device_id=device, device_id_type=MESH)

    barrier = pltpu.get_barrier_semaphore()

    @pl.when(has_up)
    def _():
        signal({"slab": up})

    @pl.when(has_down)
    def _():
        signal({"slab": down})

    @pl.when(ex == 1)
    def _():
        for o in offs:
            for e in range(2):
                signal({"ex": e, "slab": mz * gxy + xy_peer(o)})
        for o in zoffs:
            signal({"slab": lax.rem(mz + o, nz) * gxy + mxy})

    signal({"ex": 1 - ex})
    loads = [pltpu.make_async_copy(src, dst, in_sem.at[q]) for q, (src, dst) in enumerate(
        ((vol_hbm, vol), (ker_hbm, ker), (mask_hbm, mask), (cot_hbm, cot)))]
    for load in loads:
        load.start()
    lane = lax.broadcasted_iota(jnp.int32, (C, W), 1)
    first = lane == 0
    last = lane == W - 1

    def shifts(x):
        rows = x.shape[0] // C
        left, right = [], []
        for i in range(rows):
            part = x[i * C:(i + 1) * C, :].astype(F32)
            left.append(jnp.where(first, 0.0, pltpu.roll(part, 1, 1)).astype(BF16))
            right.append(jnp.where(last, 0.0, pltpu.roll(part, W - 1, 1)).astype(BF16))
        if rows == 1:
            return left[0], right[0]
        return jnp.concatenate(left, axis=0), jnp.concatenate(right, axis=0)

    def fill(layer, dz, rows):
        for r in range(*rows):
            at = flat(1 + r, 2 + r)
            x = xb[layer, dz * 3 + 1, :, at]
            if dz != 1:
                x = jnp.where(has_down if dz == 0 else has_up, x.astype(F32), 0.0).astype(BF16)
                xb[layer, dz * 3 + 1, :, at] = x
            left, right = shifts(x)
            xb[layer, dz * 3, :, at] = left
            xb[layer, dz * 3 + 2, :, at] = right

    def cols(layer, rows):
        parts = []
        for dz in range(3):
            for dh in range(3):
                for dw in range(3):
                    parts.append(xb[layer, dz * 3 + dw, :, flat(rows[0] + dh, rows[1] + dh)])
        return jnp.concatenate(parts, axis=0)

    def back_cols(layer, rows):
        parts = []
        for dh in range(3):
            for dw in range(3):
                parts.append(db[layer, dw, :, flat(rows[0] + 2 - dh, rows[1] + 2 - dh)])
        return jnp.concatenate(parts, axis=0)

    def halo_copy(layer, side, k):
        r0, r1 = spans(layer, k)
        at = flat(1 + r0, 1 + r1)
        return pltpu.make_async_remote_copy(
            src_ref=xb.at[layer, 4, :, at], dst_ref=xb.at[layer, 6 * side + 1, :, at],
            send_sem=xs_sem.at[layer, side], recv_sem=xr_sem.at[layer, side, k],
            device_id={"slab": (up, down)[side]}, device_id_type=MESH)

    def back_copy(layer, side, k):
        at = flat(0, H) if layer == 0 else flat(*spans(3, k))
        return pltpu.make_async_remote_copy(
            src_ref=bsend.at[layer, side, :, at], dst_ref=brecv.at[layer, side, :, at],
            send_sem=bs_sem.at[layer, side], recv_sem=br_sem.at[side, NC if layer == 0 else k],
            device_id={"slab": (up, down)[side]}, device_id_type=MESH)

    def start(copy, layer, k):
        @pl.when(has_up)
        def _():
            copy(layer, 0, k).start()

        @pl.when(has_down)
        def _():
            copy(layer, 1, k).start()

    def arrive(copy, layer, k):
        @pl.when(has_down)
        def _():
            copy(layer, 0, k).wait_recv()

        @pl.when(has_up)
        def _():
            copy(layer, 1, k).wait_recv()

    def sent(layer):
        for side, there in ((0, has_up), (1, has_down)):
            @pl.when(there)
            def _():
                for ref, sem in ((xb.at[layer, 4, :, flat(1, 1 + H)], xs_sem), (bsend.at[layer, side], bs_sem)):
                    pltpu.make_async_remote_copy(
                        src_ref=ref, dst_ref=ref, send_sem=sem.at[layer, side], recv_sem=br_sem.at[side, 0],
                        device_id={"slab": (up, down)[side]}, device_id_type=MESH).wait_send()

    def store_delta(layer, rows, delta):
        for i, r in enumerate(range(*rows)):
            at = flat(1 + r, 2 + r)
            x = delta[:, i * W:(i + 1) * W]
            left, right = shifts(x)
            db[layer, 1, :, at] = x
            db[layer, 2, :, at] = left
            db[layer, 0, :, at] = right

    def back(layer, rows):
        got = jnp.dot(kb[layer], back_cols(layer, rows), preferred_element_type=F32)
        at = flat(*rows)
        own[:, at] = got[C:2 * C]
        bsend[layer, 1, :, at] = got[:C].astype(BF16)
        bsend[layer, 0, :, at] = got[2 * C:].astype(BF16)

    def back_total(layer, rows):
        at = flat(*rows)
        below = jnp.where(has_down, brecv[layer, 0, :, at].astype(F32), 0.0)
        above = jnp.where(has_up, brecv[layer, 1, :, at].astype(F32), 0.0)
        return own[:, at] + below + above

    def weight_grad(layer, rows):
        d = db[layer, 1, :, flat(1 + rows[0], 1 + rows[1])]
        return lax.dot_general(d, cols(layer, rows), (((1,), (1,)), ((), ())), preferred_element_type=F32)

    loads[0].wait()
    tmp[...] = vol[...].astype(F32)
    for h in range(H):
        xb[0, 4, :, flat(1 + h, 2 + h)] = tmp[:, h, :].astype(BF16)
    zero_row = jnp.zeros((C, W), BF16)
    for edge in (0, H + 1):
        at = flat(edge, edge + 1)
        for layer in range(2):
            for q in range(9):
                xb[layer, q, :, at] = zero_row
            for q in range(3):
                db[layer, q, :C, at] = zero_row
                db[layer, q, C:, at] = zero_row
    gpad[...] = jnp.zeros_like(gpad)
    many = jnp.where(ex == 1, len(offs) + len(zoffs) + 1, len(offs) + 1)
    pl.semaphore_wait(barrier, many + has_up.astype(jnp.int32) + has_down.astype(jnp.int32))
    for k in range(NC):
        start(halo_copy, 0, k)
    fill(0, 1, (0, H))
    for load in loads[1:]:
        load.wait()
    for h in range(H):
        for q in range(2):
            row = mask[q, h:h + 1, :].astype(F32)
            mk[q, :, flat(h, h + 1)] = jnp.broadcast_to(row, (C, W))
    for layer in range(2):
        kf = ker[layer].astype(F32)
        for dh in range(3):
            for dw in range(3):
                for dz in range(3):
                    t = 9 * dz + 3 * dh + dw
                    kbt[pl.ds((dh * 3 + dw) * 2 * C, 2 * C), dz * C:(dz + 1) * C] = kf[:, t * C:(t + 1) * C]
        kb[layer] = jnp.transpose(kbt[...])[:3 * C].astype(BF16)
    tmp[...] = cot[...].astype(F32)
    chan = lax.broadcasted_iota(jnp.int32, (C, W), 0)
    weight = jnp.where(chan == canary[0], 3.0, 1.0).astype(F32)
    for h in range(H):
        dy[:, flat(h, h + 1)] = tmp[:, h, :] * scale[0] * weight

    def layer_one(rows):
        pre = jnp.dot(ker[0], cols(0, rows), preferred_element_type=F32)
        at = flat(*rows)
        pat = flat(1 + rows[0], 1 + rows[1])
        v = pre[:C]
        s = jax.nn.sigmoid(pre[C:])
        sm = s * mk[0, :, at]
        a1[:, at] = sm
        b1[:, at] = v * sm * (1.0 - s)
        xb[1, 4, :, pat] = (xb[0, 4, :, pat].astype(F32) + v * sm).astype(BF16)

    def layer_two(rows):
        pre = jnp.dot(ker[1], cols(1, rows), preferred_element_type=F32)
        at = flat(*rows)
        v = pre[:C]
        s = jax.nn.sigmoid(pre[C:])
        g = dy[:, at] * (s * mk[1, :, at])
        delta = jnp.concatenate([g, g * v * (1.0 - s)], axis=0).astype(BF16)
        store_delta(1, rows, delta)

    def spread(layer, g):
        gpad[layer, :, :27 * C] = g
        for j in range(16):
            i, n = j // 4, j % 4
            gs[layer, j // tiles, j % tiles] = gpad[layer, i * 8:(i + 1) * 8, n * W:(n + 1) * W]

    def tally(ref, send_sem, recv_sem):
        return pltpu.make_async_remote_copy(
            src_ref=ref, dst_ref=ref, send_sem=send_sem, recv_sem=recv_sem,
            device_id={"ex": 1 - ex}, device_id_type=MESH)

    def rs_copy(layer, o, e):
        r = o[1] * nx + o[0]
        peer = xy_peer(o)
        return pltpu.make_async_remote_copy(
            src_ref=gs.at[layer, peer], dst_ref=rsr.at[e, layer, r],
            send_sem=rs_s.at[layer], recv_sem=rs_r.at[e, layer],
            device_id={"ex": 1, "slab": mz * gxy + peer}, device_id_type=MESH)

    def rs_start(layer):
        for o in offs:
            rs_copy(layer, o, ex).start()

        @pl.when(ex == 0)
        def _():
            rs_copy(layer, (0, 0), 0).start()

    def z_copy(group, o):
        at = pl.ds(*groups[group])
        return pltpu.make_async_remote_copy(
            src_ref=zr.at[mz, at], dst_ref=zr.at[mz, at],
            send_sem=z_s.at[group], recv_sem=z_r.at[group],
            device_id={"slab": lax.rem(mz + o, nz) * gxy + mxy}, device_id_type=MESH)

    def z_all(group):
        return tally(zr.at[pl.ds(1, nz - 1), pl.ds(*groups[group])], z_s.at[group], z_r.at[group])

    def ag_all(group):
        return tally(ag.at[pl.ds(1, gxy - 1), pl.ds(*groups[group])], ag_s.at[group], ag_r.at[group])

    def ag_copy(group, o):
        at = pl.ds(*groups[group])
        return pltpu.make_async_remote_copy(
            src_ref=ag.at[mxy, at], dst_ref=ag.at[mxy, at],
            send_sem=ag_s.at[group], recv_sem=ag_r.at[group],
            device_id={"slab": mz * gxy + xy_peer(o)}, device_id_type=MESH)

    hand = pltpu.make_async_remote_copy(
        src_ref=kgs, dst_ref=kg_out, send_sem=p_s, recv_sem=p_r,
        device_id={"ex": 1 - ex}, device_id_type=MESH)

    def rs_total(group):
        first_slot, count = groups[group]
        for q in range(first_slot, first_slot + count):
            e, layer = slots[q]
            tally(rsr.at[e, layer, pl.ds(e, gxy - e)], rs_s.at[layer], rs_r.at[e, layer]).wait_recv()
            parts = [rsr[e, layer, r] for r in range(e, gxy)]
            if e == 1:
                parts.append(gs[layer, mxy])
            while len(parts) > 1:
                parts = [a + b for a, b in zip(parts[::2], parts[1::2])]
            zr[mz, q] = parts[0]
        for o in zoffs:
            z_copy(group, o).start()

    def z_total(group):
        first_slot, count = groups[group]
        z_all(group).wait_recv()
        for q in range(first_slot, first_slot + count):
            parts = [zr[i, q] for i in range(nz)]
            while len(parts) > 1:
                parts = [a + b for a, b in zip(parts[::2], parts[1::2])]
            ag[mxy, q] = parts[0]
        for o in offs:
            ag_copy(group, o).start()

    dx_copy = pltpu.make_async_copy(tmp, dx_out, in_sem.at[0])
    kg_copy = pltpu.make_async_copy(kgs, kg_out, in_sem.at[1])

    def input_grad():
        arrive(back_copy, 0, 0)
        for r in range(0, H, 8):
            rows = (r, r + 8)
            res = dy[:, flat(*rows)] + back_total(0, rows)
            for i in range(8):
                tmp[:, r + i, :] = res[:, i * W:(i + 1) * W]
        dx_copy.start()

    for k in range(NC):
        arrive(halo_copy, 0, k)
        fill(0, 0, spans(0, k))
        fill(0, 2, spans(0, k))
        layer_one(spans(1, k))
        start(halo_copy, 1, k)
        fill(1, 1, spans(1, k))
    for k in range(NC):
        arrive(halo_copy, 1, k)
        fill(1, 0, spans(1, k))
        fill(1, 2, spans(1, k))
        layer_two(spans(2, k))
        back(1, spans(3, k))
        start(back_copy, 1, k)
    spread(1, weight_grad(1, (0, 16)) + weight_grad(1, (16, H)))
    g1 = None
    for k in range(NC):
        rows = spans(3, k)
        at = flat(*rows)
        arrive(back_copy, 1, k)
        dx = dy[:, at] + back_total(1, rows)
        dy[:, at] = dx
        delta = jnp.concatenate([dx * a1[:, at], dx * b1[:, at]], axis=0).astype(BF16)
        store_delta(0, rows, delta)
        part = weight_grad(0, rows)
        g1 = part if k == 0 else g1 + part
        if k == NC - 2:
            rs_start(1)
    spread(0, g1)
    rs_start(0)
    for r in range(0, H, 16):
        back(0, (r, r + 16))
    start(back_copy, 0, 0)
    bound = 20.0 * float(depth * H * W) ** 0.5
    scaling = float(108 * C * C) ** 0.5 / (bound * 2.0 ** 0.5)

    def factor(e):
        square = None
        for q in range(4):
            if slots[q][0] == e:
                for j in range(16):
                    x = ag[j // tiles, q, j % tiles]
                    square = x * x if square is None else square + x * x
        norm = jnp.sqrt(jnp.sum(square, keepdims=True) + 1e-06)
        return jnp.minimum(1.0, bound / norm)

    @pl.when(ex == 1)
    def _():
        for group in range(2):
            rs_total(group)
        for group in range(2):
            z_total(group)
        input_grad()
        for group in range(2):
            ag_all(group).wait_recv()
        factors = factor(0), factor(1)
        for layer in range(2):
            for j in range(16):
                i, n = j // 4, j % 4
                width = min(W, 27 * C - n * W)
                zero, one = ag[j // tiles, 3 - layer, j % tiles], ag[j // tiles, 1 - layer, j % tiles]
                both = (zero * factors[0] + one * factors[1]) * scaling
                kgs[layer, i * 8:(i + 1) * 8, n * W:n * W + width] = both[:, :width]
        hand.start()
        kg_copy.start()
        for layer in range(2):
            tally(gs.at[layer, pl.ds(1, gxy - 1)], rs_s.at[layer], rs_r.at[1, layer]).wait_send()
        for group in range(2):
            z_all(group).wait_send()
            ag_all(group).wait_send()
        hand.wait_send()
        kg_copy.wait()

    @pl.when(ex == 0)
    def _():
        input_grad()
        for layer in range(2):
            tally(gs.at[layer], rs_s.at[layer], rs_r.at[0, layer]).wait_send()
        hand.wait_recv()

    dx_copy.wait()
    for layer in range(2):
        sent(layer)


def leave(dx_in, kg_in, dx_out, kg_out, sem):
    copies = [pltpu.make_async_copy(a, b, sem.at[i]) for i, (a, b) in enumerate(((dx_in, dx_out), (kg_in, kg_out)))]
    for copy in copies:
        copy.start()
    for copy in copies:
        copy.wait()


def in_hbm(x):
    return pltpu.with_memory_space_constraint(x, pltpu.HBM)


def per_device(volume, cotangent, gate_mask, loss_scale, canary, kernels):
    slabs = lax.axis_size("slab")
    torus = torus_of(slabs)
    nx, ny, nz = torus
    gxy = nx * ny
    part = (16 // gxy, 8, W)
    sm = pl.BlockSpec(memory_space=pltpu.SMEM)
    hbm = pl.BlockSpec(memory_space=pltpu.HBM)
    anywhere = pl.BlockSpec(memory_space=pl.ANY)
    dma = pltpu.SemaphoreType.DMA
    shapes = (jax.ShapeDtypeStruct((C, H, W), F32), jax.ShapeDtypeStruct((2, 2 * C, 27 * C), F32))
    dx, kg = pl.pallas_call(
        functools.partial(kernel, torus, slabs),
        out_shape=shapes,
        in_specs=[hbm, hbm, hbm, sm, sm, hbm],
        out_specs=(anywhere, anywhere),
        scratch_shapes=[
            pltpu.VMEM((C, H, W), BF16),
            pltpu.VMEM((C, H, W), BF16),
            pltpu.VMEM((2, H, W), jnp.int32),
            pltpu.VMEM((2, 2 * C, 27 * C), BF16),
            pltpu.VMEM((C, H, W), F32),
            pltpu.VMEM((2, 9, C, PW), BF16),
            pltpu.VMEM((2, 3, 2 * C, PW), BF16),
            pltpu.VMEM((18 * C, W), F32),
            pltpu.VMEM((2, 3 * C, 18 * C), BF16),
            pltpu.VMEM((2, C, H * W), F32),
            pltpu.VMEM((C, H * W), F32),
            pltpu.VMEM((C, H * W), F32),
            pltpu.VMEM((C, H * W), F32),
            pltpu.VMEM((C, H * W), F32),
            pltpu.VMEM((2, 2, C, H * W), BF16),
            pltpu.VMEM((2, 2, C, H * W), BF16),
            pltpu.VMEM((2, 2 * C, 4 * W), F32),
            pltpu.VMEM((2, gxy) + part, F32),
            pltpu.VMEM((2, 2, gxy) + part, F32),
            pltpu.VMEM((nz, 4) + part, F32),
            pltpu.VMEM((gxy, 4) + part, F32),
            pltpu.VMEM((2, 2 * C, 27 * C), F32),
            dma((2, 2)), dma((2, 2, NC)), dma((2, 2)), dma((2, NC + 1)),
            dma((2,)), dma((2, 2)), dma((2,)), dma((2,)), dma((2,)), dma((2,)),
            dma, dma, dma((4,)),
        ],
        compiler_params=pltpu.CompilerParams(
            collective_id=0, has_side_effects=True, vmem_limit_bytes=48 * 1024 * 1024),
        name="gated_level",
    )(
        in_hbm(volume.reshape((C, H, W))),
        in_hbm(cotangent.reshape((C, H, W))),
        in_hbm(gate_mask.reshape((2, H, W))),
        loss_scale,
        canary,
        in_hbm(kernels),
    )
    dx, kg = pl.pallas_call(
        leave,
        out_shape=shapes,
        in_specs=[anywhere, anywhere],
        out_specs=(hbm, hbm),
        scratch_shapes=[dma((2,))],
        compiler_params=pltpu.CompilerParams(vmem_limit_bytes=1024 * 1024),
        name="leave",
    )(dx, kg)
    return dx.reshape((1, C, 1, H, W)), kg


def solution(mesh):
    placed = (
        P("ex", None, "slab", None, None),
        P("ex", None, "slab", None, None),
        P("ex", None, "slab", None, None),
        P("ex"),
        P("ex"),
        P(),
    )
    return jax.shard_map(
        per_device,
        mesh=mesh,
        in_specs=placed,
        out_specs=(P("ex", None, "slab", None, None), P()),
        check_vma=False,
    )
```

```python
import functools
import jax
import jax.numpy as jnp
from jax import lax
from jax.experimental import pallas as pl
from jax.experimental.pallas import tpu as pltpu
from jax.sharding import PartitionSpec as P

F32 = jnp.float32
BF16 = jnp.bfloat16
MESH = pl.DeviceIdType.MESH
C = 16
H = 32
W = 128
PW = (H + 2) * W
ROWS = (
    (0, 8, 16, 23, 29, 32),
    (0, 7, 15, 22, 28, 32),
    (0, 6, 14, 21, 27, 32),
    (0, 5, 13, 20, 26, 32),
)
NC = len(ROWS[0]) - 1


def torus_of(slabs):
    return {128: (4, 4, 8), 8: (2, 2, 2)}[slabs]


def owners_of(slabs):
    return {128: tuple((x, y) for y in range(4) for x in range(4)), 8: ((0, 0), (1, 0), (0, 1), (1, 1))}[slabs]


def spans(stage, k):
    return ROWS[stage][k], ROWS[stage][k + 1]


def flat(r0, r1):
    return pl.ds(r0 * W, (r1 - r0) * W)


def kernel(torus, depth, vol_hbm, cot_hbm, mask_hbm, scale, canary, ker_hbm, dx_out, kg_out,
           vol, cot, mask, ker, tmp, xb, db, kbt, kb, mk, a1, b1, dy, own, bsend, brecv, gpad,
           gs, rsr, zr, ag,
           xs_sem, xr_sem, bs_sem, br_sem, rs_s, rs_r, z_s, z_r, ag_s, ag_r, p_s, p_r, in_sem):
    nx, ny, nz = torus
    gxy = nx * ny
    slabs = gxy * nz
    me = lax.axis_index("slab")
    ex = lax.axis_index("ex")
    mz = me // gxy
    mxy = lax.rem(me, gxy)
    my = mxy // nx
    mx = lax.rem(mxy, nx)
    offs = [(a, b) for b in range(ny) for a in range(nx) if (a, b) != (0, 0)]
    offs.sort(key=lambda o: -(min(o[0], nx - o[0]) + min(o[1], ny - o[1])))
    zoffs = sorted(range(1, nz), key=lambda o: -min(o, nz - o))
    owners = owners_of(slabs)
    held = len(owners)
    tiles = 16 // held
    slots = ((1, 1), (0, 1), (1, 0), (0, 0))
    groups = ((0, 2), (2, 1), (3, 1))
    mine = [((mx == a) & (my == b)).astype(jnp.int32) for a, b in owners]
    owns = sum(mine)
    mo = sum(i * m for i, m in enumerate(mine))
    is_owner = owns > 0
    has_down = me > 0
    has_up = me < slabs - 1
    up = jnp.minimum(me + 1, slabs - 1)
    down = jnp.maximum(me - 1, 0)

    def xy_peer(o):
        return lax.rem(my + o[1], ny) * nx + lax.rem(mx + o[0], nx)

    def signal(device):
        pl.semaphore_signal(barrier, inc=1, device_id=device, device_id_type=MESH)

    barrier = pltpu.get_barrier_semaphore()

    @pl.when(has_up)
    def _():
        signal({"slab": up})

    @pl.when(has_down)
    def _():
        signal({"slab": down})

    @pl.when((ex == 1) & is_owner)
    def _():
        for o in offs:
            for e in range(2):
                signal({"ex": e, "slab": mz * gxy + xy_peer(o)})
        for o in zoffs:
            signal({"slab": lax.rem(mz + o, nz) * gxy + mxy})

    @pl.when((ex == 1) & jnp.logical_not(is_owner))
    def _():
        for a, b in owners:
            signal({"slab": mz * gxy + b * nx + a})

    signal({"ex": 1 - ex})
    loads = [pltpu.make_async_copy(src, dst, in_sem.at[q]) for q, (src, dst) in enumerate(
        ((vol_hbm, vol), (ker_hbm, ker), (mask_hbm, mask), (cot_hbm, cot)))]
    for load in loads:
        load.start()
    lane = lax.broadcasted_iota(jnp.int32, (C, W), 1)
    first = lane == 0
    last = lane == W - 1

    keep_right = jnp.where(first, 0.0, 1.0).astype(BF16)
    keep_left = jnp.where(last, 0.0, 1.0).astype(BF16)

    def shifts(x):
        left, right = [], []
        for i in range(x.shape[0] // C):
            part = x[i * C:(i + 1) * C, :]
            left.append(pltpu.roll(part, 1, 1) * keep_right)
            right.append(pltpu.roll(part, W - 1, 1) * keep_left)
        if len(left) == 1:
            return left[0], right[0]
        return jnp.concatenate(left, axis=0), jnp.concatenate(right, axis=0)

    def fill(layer, dz, rows):
        for r in range(*rows):
            at = flat(1 + r, 2 + r)
            x = xb[layer, dz * 3 + 1, :, at]
            if dz != 1:
                x = jnp.where(has_down if dz == 0 else has_up, x.astype(F32), 0.0).astype(BF16)
                xb[layer, dz * 3 + 1, :, at] = x
            left, right = shifts(x)
            xb[layer, dz * 3, :, at] = left
            xb[layer, dz * 3 + 2, :, at] = right

    def cols(layer, rows):
        parts = []
        for dz in range(3):
            for dh in range(3):
                for dw in range(3):
                    parts.append(xb[layer, dz * 3 + dw, :, flat(rows[0] + dh, rows[1] + dh)])
        return jnp.concatenate(parts, axis=0)

    def back_cols(layer, rows):
        parts = []
        for dh in range(3):
            for dw in range(3):
                parts.append(db[layer, dw, :, flat(rows[0] + 2 - dh, rows[1] + 2 - dh)])
        return jnp.concatenate(parts, axis=0)

    def halo_copy(layer, side, k):
        r0, r1 = spans(layer, k)
        at = flat(1 + r0, 1 + r1)
        return pltpu.make_async_remote_copy(
            src_ref=xb.at[layer, 4, :, at], dst_ref=xb.at[layer, 6 * side + 1, :, at],
            send_sem=xs_sem.at[layer, side], recv_sem=xr_sem.at[layer, side, k],
            device_id={"slab": (up, down)[side]}, device_id_type=MESH)

    def back_copy(layer, side, k):
        at = flat(0, H) if layer == 0 else flat(*spans(3, k))
        return pltpu.make_async_remote_copy(
            src_ref=bsend.at[layer, side, :, at], dst_ref=brecv.at[layer, side, :, at],
            send_sem=bs_sem.at[layer, side], recv_sem=br_sem.at[side, NC if layer == 0 else k],
            device_id={"slab": (up, down)[side]}, device_id_type=MESH)

    def start(copy, layer, k):
        @pl.when(has_up)
        def _():
            copy(layer, 0, k).start()

        @pl.when(has_down)
        def _():
            copy(layer, 1, k).start()

    def arrive(copy, layer, k):
        @pl.when(has_down)
        def _():
            copy(layer, 0, k).wait_recv()

        @pl.when(has_up)
        def _():
            copy(layer, 1, k).wait_recv()

    def sent(layer):
        for side, there in ((0, has_up), (1, has_down)):
            @pl.when(there)
            def _():
                for ref, sem in ((xb.at[layer, 4, :, flat(1, 1 + H)], xs_sem), (bsend.at[layer, side], bs_sem)):
                    pltpu.make_async_remote_copy(
                        src_ref=ref, dst_ref=ref, send_sem=sem.at[layer, side], recv_sem=br_sem.at[side, 0],
                        device_id={"slab": (up, down)[side]}, device_id_type=MESH).wait_send()

    def store_delta(layer, rows, delta):
        for i, r in enumerate(range(*rows)):
            at = flat(1 + r, 2 + r)
            x = delta[:, i * W:(i + 1) * W]
            left, right = shifts(x)
            db[layer, 1, :, at] = x
            db[layer, 2, :, at] = left
            db[layer, 0, :, at] = right

    def back(layer, rows):
        got = jnp.dot(kb[layer], back_cols(layer, rows), preferred_element_type=F32)
        at = flat(*rows)
        own[:, at] = got[C:2 * C]
        bsend[layer, 1, :, at] = got[:C].astype(BF16)
        bsend[layer, 0, :, at] = got[2 * C:].astype(BF16)

    def back_total(layer, rows):
        at = flat(*rows)
        below = jnp.where(has_down, brecv[layer, 0, :, at].astype(F32), 0.0)
        above = jnp.where(has_up, brecv[layer, 1, :, at].astype(F32), 0.0)
        return own[:, at] + below + above

    def weight_grad(layer, rows):
        d = db[layer, 1, :, flat(1 + rows[0], 1 + rows[1])]
        return lax.dot_general(d, cols(layer, rows), (((1,), (1,)), ((), ())), preferred_element_type=F32)

    loads[0].wait()
    tmp[...] = vol[...].astype(F32)
    for h in range(H):
        xb[0, 4, :, flat(1 + h, 2 + h)] = tmp[:, h, :].astype(BF16)
    zero_row = jnp.zeros((C, W), BF16)
    for edge in (0, H + 1):
        at = flat(edge, edge + 1)
        for layer in range(2):
            for q in range(9):
                xb[layer, q, :, at] = zero_row
            for q in range(3):
                db[layer, q, :C, at] = zero_row
                db[layer, q, C:, at] = zero_row
    gpad[...] = jnp.zeros_like(gpad)
    many = 1 + jnp.where(
        ex == 1, jnp.where(is_owner, len(offs) + len(zoffs), held), held - owns)
    pl.semaphore_wait(barrier, many + has_up.astype(jnp.int32) + has_down.astype(jnp.int32))
    for k in range(NC):
        start(halo_copy, 0, k)
    fill(0, 1, (0, H))
    for load in loads[1:]:
        load.wait()
    for h in range(H):
        for q in range(2):
            row = mask[q, h:h + 1, :].astype(F32)
            mk[q, :, flat(h, h + 1)] = jnp.broadcast_to(row, (C, W))
    for layer in range(2):
        kf = ker[layer].astype(F32)
        for dh in range(3):
            for dw in range(3):
                for dz in range(3):
                    t = 9 * dz + 3 * dh + dw
                    kbt[pl.ds((dh * 3 + dw) * 2 * C, 2 * C), dz * C:(dz + 1) * C] = kf[:, t * C:(t + 1) * C]
        kb[layer] = jnp.transpose(kbt[...])[:3 * C].astype(BF16)
    tmp[...] = cot[...].astype(F32)
    chan = lax.broadcasted_iota(jnp.int32, (C, W), 0)
    weight = jnp.where(chan == canary[0], 3.0, 1.0).astype(F32)
    for h in range(H):
        dy[:, flat(h, h + 1)] = tmp[:, h, :] * scale[0] * weight

    def layer_one(rows):
        pre = jnp.dot(ker[0], cols(0, rows), preferred_element_type=F32)
        at = flat(*rows)
        pat = flat(1 + rows[0], 1 + rows[1])
        v = pre[:C]
        s = jax.nn.sigmoid(pre[C:])
        sm = s * mk[0, :, at]
        a1[:, at] = sm
        b1[:, at] = v * sm * (1.0 - s)
        xb[1, 4, :, pat] = (xb[0, 4, :, pat].astype(F32) + v * sm).astype(BF16)

    def layer_two(rows):
        pre = jnp.dot(ker[1], cols(1, rows), preferred_element_type=F32)
        at = flat(*rows)
        v = pre[:C]
        s = jax.nn.sigmoid(pre[C:])
        g = dy[:, at] * (s * mk[1, :, at])
        delta = jnp.concatenate([g, g * v * (1.0 - s)], axis=0).astype(BF16)
        store_delta(1, rows, delta)

    def spread(layer, g):
        gpad[layer, :, :27 * C] = g
        for j in range(16):
            i, n = j // 4, j % 4
            gs[layer, j // tiles, j % tiles] = gpad[layer, i * 8:(i + 1) * 8, n * W:(n + 1) * W]

    def tally(ref, send_sem, recv_sem):
        return pltpu.make_async_remote_copy(
            src_ref=ref, dst_ref=ref, send_sem=send_sem, recv_sem=recv_sem,
            device_id={"ex": 1 - ex}, device_id_type=MESH)

    def rs_start(layer):
        for i, (a, b) in enumerate(owners):
            copy = pltpu.make_async_remote_copy(
                src_ref=gs.at[layer, i], dst_ref=rsr.at[ex, layer, mxy],
                send_sem=rs_s.at[layer], recv_sem=rs_r.at[ex, layer],
                device_id={"ex": 1, "slab": mz * gxy + b * nx + a}, device_id_type=MESH)

            @pl.when((ex == 0) | (mine[i] == 0))
            def _():
                copy.start()

    def z_copy(group, o):
        at = pl.ds(*groups[group])
        return pltpu.make_async_remote_copy(
            src_ref=zr.at[mz, at], dst_ref=zr.at[mz, at],
            send_sem=z_s.at[group], recv_sem=z_r.at[group],
            device_id={"slab": lax.rem(mz + o, nz) * gxy + mxy}, device_id_type=MESH)

    def z_all(group):
        return tally(zr.at[pl.ds(1, nz - 1), pl.ds(*groups[group])], z_s.at[group], z_r.at[group])

    def ag_all(group, count):
        return tally(ag.at[pl.ds(0, count), pl.ds(*groups[group])], ag_s.at[group], ag_r.at[group])

    def ag_copy(group, o):
        at = pl.ds(*groups[group])
        return pltpu.make_async_remote_copy(
            src_ref=ag.at[mo, at], dst_ref=ag.at[mo, at],
            send_sem=ag_s.at[group], recv_sem=ag_r.at[group],
            device_id={"slab": mz * gxy + xy_peer(o)}, device_id_type=MESH)

    hand = pltpu.make_async_remote_copy(
        src_ref=kg_out, dst_ref=kg_out, send_sem=p_s, recv_sem=p_r,
        device_id={"ex": 1 - ex}, device_id_type=MESH)

    def rs_total(group):
        first_slot, count = groups[group]
        for q in range(first_slot, first_slot + count):
            e, layer = slots[q]
            if e == 1:
                rsr[1, layer, mxy] = gs[layer, mo]
            tally(rsr.at[e, layer, pl.ds(e, gxy - e)], rs_s.at[layer], rs_r.at[e, layer]).wait_recv()
            parts = [rsr[e, layer, r] for r in range(gxy)]
            while len(parts) > 1:
                parts = [a + b for a, b in zip(parts[::2], parts[1::2])]
            zr[mz, q] = parts[0]
        for o in zoffs:
            z_copy(group, o).start()

    def z_total(group):
        first_slot, count = groups[group]
        z_all(group).wait_recv()
        for q in range(first_slot, first_slot + count):
            parts = [zr[i, q] for i in range(nz)]
            while len(parts) > 1:
                parts = [a + b for a, b in zip(parts[::2], parts[1::2])]
            ag[mo, q] = parts[0]
        for o in offs:
            ag_copy(group, o).start()

    def input_grad():
        arrive(back_copy, 0, 0)
        for r in range(0, H, 8):
            rows = (r, r + 8)
            res = dy[:, flat(*rows)] + back_total(0, rows)
            for i in range(8):
                dx_out[:, r + i, :] = res[:, i * W:(i + 1) * W]

    for k in range(NC):
        arrive(halo_copy, 0, k)
        fill(0, 0, spans(0, k))
        fill(0, 2, spans(0, k))
        layer_one(spans(1, k))
        start(halo_copy, 1, k)
    fill(1, 1, (0, H))
    for k in range(NC):
        arrive(halo_copy, 1, k)
        fill(1, 0, spans(1, k))
        fill(1, 2, spans(1, k))
        layer_two(spans(2, k))
        back(1, spans(3, k))
        start(back_copy, 1, k)
    spread(1, weight_grad(1, (0, 16)) + weight_grad(1, (16, H)))
    g1 = None
    for k in range(NC):
        rows = spans(3, k)
        at = flat(*rows)
        arrive(back_copy, 1, k)
        dx = dy[:, at] + back_total(1, rows)
        dy[:, at] = dx
        delta = jnp.concatenate([dx * a1[:, at], dx * b1[:, at]], axis=0).astype(BF16)
        store_delta(0, rows, delta)
        part = weight_grad(0, rows)
        g1 = part if k == 0 else g1 + part
        if k == NC - 2:
            rs_start(1)
    spread(0, g1)
    rs_start(0)
    for r in range(0, H, 16):
        back(0, (r, r + 16))
    start(back_copy, 0, 0)
    bound = 20.0 * float(depth * H * W) ** 0.5
    scaling = float(108 * C * C) ** 0.5 / (bound * 2.0 ** 0.5)

    def factor(e):
        square = None
        for q in range(4):
            if slots[q][0] == e:
                for j in range(16):
                    x = ag[j // tiles, q, j % tiles]
                    square = x * x if square is None else square + x * x
        norm = jnp.sqrt(jnp.sum(square, keepdims=True) + 1e-06)
        return jnp.minimum(1.0, bound / norm)

    @pl.when((ex == 1) & is_owner)
    def _():
        for group in range(len(groups)):
            rs_total(group)
        for group in range(len(groups)):
            z_total(group)

    @pl.when(ex == 1)
    def _():
        input_grad()

        @pl.when(is_owner)
        def _():
            for group in range(len(groups)):
                ag_all(group, held - 1).wait_recv()

        @pl.when(jnp.logical_not(is_owner))
        def _():
            for group in range(len(groups)):
                ag_all(group, held).wait_recv()

        factors = factor(0), factor(1)
        for layer in range(2):
            for j in range(16):
                i, n = j // 4, j % 4
                width = min(W, 27 * C - n * W)
                zero, one = (ag[j // tiles, slots.index((e, layer)), j % tiles] for e in range(2))
                both = (zero * factors[0] + one * factors[1]) * scaling
                kg_out[layer, i * 8:(i + 1) * 8, n * W:n * W + width] = both[:, :width]
        hand.start()
        @pl.when(is_owner)
        def _():
            for layer in range(2):
                tally(gs.at[layer, pl.ds(1, held - 1)], rs_s.at[layer], rs_r.at[1, layer]).wait_send()
            for group in range(len(groups)):
                z_all(group).wait_send()
                tally(ag.at[pl.ds(0, gxy - 1), pl.ds(*groups[group])], ag_s.at[group], ag_r.at[group]).wait_send()

        @pl.when(jnp.logical_not(is_owner))
        def _():
            for layer in range(2):
                tally(gs.at[layer], rs_s.at[layer], rs_r.at[1, layer]).wait_send()

        hand.wait_send()

    @pl.when(ex == 0)
    def _():
        input_grad()
        for layer in range(2):
            tally(gs.at[layer], rs_s.at[layer], rs_r.at[0, layer]).wait_send()
        hand.wait_recv()

    for layer in range(2):
        sent(layer)


def leave(dx_in, kg_in, dx_out, kg_out, sem):
    copies = [pltpu.make_async_copy(a, b, sem.at[i]) for i, (a, b) in enumerate(((dx_in, dx_out), (kg_in, kg_out)))]
    for copy in copies:
        copy.start()
    for copy in copies:
        copy.wait()


def in_hbm(x):
    return pltpu.with_memory_space_constraint(x, pltpu.HBM)


def per_device(volume, cotangent, gate_mask, loss_scale, canary, kernels):
    slabs = lax.axis_size("slab")
    torus = torus_of(slabs)
    nx, ny, nz = torus
    gxy = nx * ny
    held = len(owners_of(slabs))
    part = (16 // held, 8, W)
    sm = pl.BlockSpec(memory_space=pltpu.SMEM)
    hbm = pl.BlockSpec(memory_space=pltpu.HBM)
    anywhere = pl.BlockSpec(memory_space=pl.ANY)
    vm = pl.BlockSpec(memory_space=pltpu.VMEM)
    dma = pltpu.SemaphoreType.DMA
    shapes = (jax.ShapeDtypeStruct((C, H, W), F32), jax.ShapeDtypeStruct((2, 2 * C, 27 * C), F32))
    dx, kg = pl.pallas_call(
        functools.partial(kernel, torus, slabs),
        out_shape=shapes,
        in_specs=[hbm, hbm, hbm, sm, sm, hbm],
        out_specs=(vm, vm),
        scratch_shapes=[
            pltpu.VMEM((C, H, W), BF16),
            pltpu.VMEM((C, H, W), BF16),
            pltpu.VMEM((2, H, W), jnp.int32),
            pltpu.VMEM((2, 2 * C, 27 * C), BF16),
            pltpu.VMEM((C, H, W), F32),
            pltpu.VMEM((2, 9, C, PW), BF16),
            pltpu.VMEM((2, 3, 2 * C, PW), BF16),
            pltpu.VMEM((18 * C, W), F32),
            pltpu.VMEM((2, 3 * C, 18 * C), BF16),
            pltpu.VMEM((2, C, H * W), F32),
            pltpu.VMEM((C, H * W), F32),
            pltpu.VMEM((C, H * W), F32),
            pltpu.VMEM((C, H * W), F32),
            pltpu.VMEM((C, H * W), F32),
            pltpu.VMEM((2, 2, C, H * W), BF16),
            pltpu.VMEM((2, 2, C, H * W), BF16),
            pltpu.VMEM((2, 2 * C, 4 * W), F32),
            pltpu.VMEM((2, held) + part, F32),
            pltpu.VMEM((2, 2, gxy) + part, F32),
            pltpu.VMEM((nz, 4) + part, F32),
            pltpu.VMEM((held, 4) + part, F32),
            dma((2, 2)), dma((2, 2, NC)), dma((2, 2)), dma((2, NC + 1)),
            dma((2,)), dma((2, 2)), dma((3,)), dma((3,)), dma((3,)), dma((3,)),
            dma, dma, dma((4,)),
        ],
        compiler_params=pltpu.CompilerParams(
            collective_id=0, has_side_effects=True, vmem_limit_bytes=48 * 1024 * 1024),
        name="gated_level",
    )(
        in_hbm(volume.reshape((C, H, W))),
        in_hbm(cotangent.reshape((C, H, W))),
        in_hbm(gate_mask.reshape((2, H, W))),
        loss_scale,
        canary,
        in_hbm(kernels),
    )
    dx, kg = pl.pallas_call(
        leave,
        out_shape=shapes,
        in_specs=[anywhere, anywhere],
        out_specs=(hbm, hbm),
        scratch_shapes=[dma((2,))],
        compiler_params=pltpu.CompilerParams(vmem_limit_bytes=1024 * 1024),
        name="leave",
    )(dx, kg)
    return dx.reshape((1, C, 1, H, W)), kg


def solution(mesh):
    placed = (
        P("ex", None, "slab", None, None),
        P("ex", None, "slab", None, None),
        P("ex", None, "slab", None, None),
        P("ex"),
        P("ex"),
        P(),
    )
    return jax.shard_map(
        per_device,
        mesh=mesh,
        in_specs=placed,
        out_specs=(P("ex", None, "slab", None, None), P()),
        check_vma=False,
    )
```

```python
import functools
import jax
import jax.numpy as jnp
from jax import lax
from jax.experimental import pallas as pl
from jax.experimental.pallas import tpu as pltpu
from jax.sharding import PartitionSpec as P

F32 = jnp.float32
BF16 = jnp.bfloat16
MESH = pl.DeviceIdType.MESH
C = 16
H = 32
W = 128
PW = (H + 2) * W
ROWS = (
    (0, 8, 16, 23, 29, 32),
    (0, 7, 15, 22, 28, 32),
    (0, 6, 14, 21, 27, 32),
    (0, 5, 13, 20, 26, 32),
)
NC = len(ROWS[0]) - 1


def torus_of(slabs):
    return {128: (4, 4, 8), 8: (2, 2, 2)}[slabs]


def owners_of(slabs):
    return {128: tuple((x, y) for y in range(4) for x in range(4)), 8: ((0, 0), (1, 0), (0, 1), (1, 1))}[slabs]


def spans(stage, k):
    return ROWS[stage][k], ROWS[stage][k + 1]


def flat(r0, r1):
    return pl.ds(r0 * W, (r1 - r0) * W)


def kernel(torus, depth, vol_hbm, cot_hbm, mask_hbm, scale, canary, ker_hbm, dx_out, kg_out,
           vol, cot, mask, ker, tmp, xb, db, kbt, kb, mk, a1, b1, dy, own, bsend, brecv, gpad,
           gs, rsr, zr, ag,
           xs_sem, xr_sem, bs_sem, br_sem, rs_s, rs_r, z_s, z_r, ag_s, ag_r, p_s, p_r, in_sem):
    nx, ny, nz = torus
    gxy = nx * ny
    slabs = gxy * nz
    me = lax.axis_index("slab")
    ex = lax.axis_index("ex")
    mz = me // gxy
    mxy = lax.rem(me, gxy)
    my = mxy // nx
    mx = lax.rem(mxy, nx)
    offs = [(a, b) for b in range(ny) for a in range(nx) if (a, b) != (0, 0)]
    offs.sort(key=lambda o: -(min(o[0], nx - o[0]) + min(o[1], ny - o[1])))
    zoffs = sorted(range(1, nz), key=lambda o: -min(o, nz - o))
    owners = owners_of(slabs)
    held = len(owners)
    tiles = 16 // held
    slots = ((1, 1), (0, 1), (1, 0), (0, 0))
    groups = ((0, 2), (2, 1), (3, 1))
    mine = [((mx == a) & (my == b)).astype(jnp.int32) for a, b in owners]
    owns = sum(mine)
    mo = sum(i * m for i, m in enumerate(mine))
    is_owner = owns > 0
    has_down = me > 0
    has_up = me < slabs - 1
    up = jnp.minimum(me + 1, slabs - 1)
    down = jnp.maximum(me - 1, 0)

    def xy_peer(o):
        return lax.rem(my + o[1], ny) * nx + lax.rem(mx + o[0], nx)

    def signal(device):
        pl.semaphore_signal(barrier, inc=1, device_id=device, device_id_type=MESH)

    barrier = pltpu.get_barrier_semaphore()

    @pl.when(has_up)
    def _():
        signal({"slab": up})

    @pl.when(has_down)
    def _():
        signal({"slab": down})

    @pl.when((ex == 1) & is_owner)
    def _():
        for o in offs:
            for e in range(2):
                signal({"ex": e, "slab": mz * gxy + xy_peer(o)})
        for o in zoffs:
            signal({"slab": lax.rem(mz + o, nz) * gxy + mxy})

    @pl.when((ex == 1) & jnp.logical_not(is_owner))
    def _():
        for a, b in owners:
            signal({"slab": mz * gxy + b * nx + a})

    signal({"ex": 1 - ex})
    loads = [pltpu.make_async_copy(src, dst, in_sem.at[q]) for q, (src, dst) in enumerate(
        ((vol_hbm, vol), (ker_hbm, ker), (mask_hbm, mask), (cot_hbm, cot)))]
    for load in loads:
        load.start()
    lane = lax.broadcasted_iota(jnp.int32, (C, W), 1)
    first = lane == 0
    last = lane == W - 1

    keep_right = jnp.where(first, 0.0, 1.0).astype(BF16)
    keep_left = jnp.where(last, 0.0, 1.0).astype(BF16)

    def shifts(x):
        left, right = [], []
        for i in range(x.shape[0] // C):
            part = x[i * C:(i + 1) * C, :]
            left.append(pltpu.roll(part, 1, 1) * keep_right)
            right.append(pltpu.roll(part, W - 1, 1) * keep_left)
        if len(left) == 1:
            return left[0], right[0]
        return jnp.concatenate(left, axis=0), jnp.concatenate(right, axis=0)

    def fill(layer, dz, rows):
        for r in range(*rows):
            at = flat(1 + r, 2 + r)
            x = xb[layer, dz * 3 + 1, :, at]
            if dz != 1:
                x = jnp.where(has_down if dz == 0 else has_up, x.astype(F32), 0.0).astype(BF16)
                xb[layer, dz * 3 + 1, :, at] = x
            left, right = shifts(x)
            xb[layer, dz * 3, :, at] = left
            xb[layer, dz * 3 + 2, :, at] = right

    def cols(layer, rows):
        parts = []
        for dz in range(3):
            for dh in range(3):
                for dw in range(3):
                    parts.append(xb[layer, dz * 3 + dw, :, flat(rows[0] + dh, rows[1] + dh)])
        return jnp.concatenate(parts, axis=0)

    def back_cols(layer, rows):
        parts = []
        for dh in range(3):
            for dw in range(3):
                parts.append(db[layer, dw, :, flat(rows[0] + 2 - dh, rows[1] + 2 - dh)])
        return jnp.concatenate(parts, axis=0)

    def halo_copy(layer, side, k):
        r0, r1 = spans(layer, k)
        at = flat(1 + r0, 1 + r1)
        return pltpu.make_async_remote_copy(
            src_ref=xb.at[layer, 4, :, at], dst_ref=xb.at[layer, 6 * side + 1, :, at],
            send_sem=xs_sem.at[layer, side], recv_sem=xr_sem.at[layer, side, k],
            device_id={"slab": (up, down)[side]}, device_id_type=MESH)

    def back_copy(layer, side, k):
        at = flat(0, H) if layer == 0 else flat(*spans(3, k))
        return pltpu.make_async_remote_copy(
            src_ref=bsend.at[layer, side, :, at], dst_ref=brecv.at[layer, side, :, at],
            send_sem=bs_sem.at[layer, side], recv_sem=br_sem.at[side, NC if layer == 0 else k],
            device_id={"slab": (up, down)[side]}, device_id_type=MESH)

    def start(copy, layer, k):
        @pl.when(has_up)
        def _():
            copy(layer, 0, k).start()

        @pl.when(has_down)
        def _():
            copy(layer, 1, k).start()

    def arrive(copy, layer, k):
        @pl.when(has_down)
        def _():
            copy(layer, 0, k).wait_recv()

        @pl.when(has_up)
        def _():
            copy(layer, 1, k).wait_recv()

    def sent(layer):
        for side, there in ((0, has_up), (1, has_down)):
            @pl.when(there)
            def _():
                for ref, sem in ((xb.at[layer, 4, :, flat(1, 1 + H)], xs_sem), (bsend.at[layer, side], bs_sem)):
                    pltpu.make_async_remote_copy(
                        src_ref=ref, dst_ref=ref, send_sem=sem.at[layer, side], recv_sem=br_sem.at[side, 0],
                        device_id={"slab": (up, down)[side]}, device_id_type=MESH).wait_send()

    def store_delta(layer, rows, delta):
        for i, r in enumerate(range(*rows)):
            at = flat(1 + r, 2 + r)
            x = delta[:, i * W:(i + 1) * W]
            left, right = shifts(x)
            db[layer, 1, :, at] = x
            db[layer, 2, :, at] = left
            db[layer, 0, :, at] = right

    def back(layer, rows):
        got = jnp.dot(kb[layer], back_cols(layer, rows), preferred_element_type=F32)
        at = flat(*rows)
        own[:, at] = got[C:2 * C]
        bsend[layer, 1, :, at] = got[:C].astype(BF16)
        bsend[layer, 0, :, at] = got[2 * C:].astype(BF16)

    def back_total(layer, rows):
        at = flat(*rows)
        below = jnp.where(has_down, brecv[layer, 0, :, at].astype(F32), 0.0)
        above = jnp.where(has_up, brecv[layer, 1, :, at].astype(F32), 0.0)
        return own[:, at] + below + above

    def weight_grad(layer, rows):
        d = db[layer, 1, :, flat(1 + rows[0], 1 + rows[1])]
        return lax.dot_general(d, cols(layer, rows), (((1,), (1,)), ((), ())), preferred_element_type=F32)

    loads[0].wait()
    tmp[...] = vol[...].astype(F32)
    for h in range(H):
        xb[0, 4, :, flat(1 + h, 2 + h)] = tmp[:, h, :].astype(BF16)
    zero_row = jnp.zeros((C, W), BF16)
    for edge in (0, H + 1):
        at = flat(edge, edge + 1)
        for layer in range(2):
            for q in range(9):
                xb[layer, q, :, at] = zero_row
            for q in range(3):
                db[layer, q, :C, at] = zero_row
                db[layer, q, C:, at] = zero_row
    gpad[...] = jnp.zeros_like(gpad)
    many = 1 + jnp.where(
        ex == 1, jnp.where(is_owner, len(offs) + len(zoffs), held), held - owns)
    pl.semaphore_wait(barrier, many + has_up.astype(jnp.int32) + has_down.astype(jnp.int32))
    for k in range(NC):
        start(halo_copy, 0, k)
    fill(0, 1, (0, H))
    for load in loads[1:]:
        load.wait()
    for h in range(H):
        for q in range(2):
            row = mask[q, h:h + 1, :].astype(F32)
            mk[q, :, flat(h, h + 1)] = jnp.broadcast_to(row, (C, W))
    for layer in range(2):
        kf = ker[layer].astype(F32)
        for dh in range(3):
            for dw in range(3):
                for dz in range(3):
                    t = 9 * dz + 3 * dh + dw
                    kbt[pl.ds((dh * 3 + dw) * 2 * C, 2 * C), dz * C:(dz + 1) * C] = kf[:, t * C:(t + 1) * C]
        kb[layer] = jnp.transpose(kbt[...])[:3 * C].astype(BF16)
    tmp[...] = cot[...].astype(F32)
    chan = lax.broadcasted_iota(jnp.int32, (C, W), 0)
    weight = jnp.where(chan == canary[0], 3.0, 1.0).astype(F32)
    for h in range(H):
        dy[:, flat(h, h + 1)] = tmp[:, h, :] * scale[0] * weight

    def layer_one(rows):
        pre = jnp.dot(ker[0], cols(0, rows), preferred_element_type=F32)
        at = flat(*rows)
        pat = flat(1 + rows[0], 1 + rows[1])
        v = pre[:C]
        s = jax.nn.sigmoid(pre[C:])
        sm = s * mk[0, :, at]
        a1[:, at] = sm
        b1[:, at] = v * sm * (1.0 - s)
        xb[1, 4, :, pat] = (xb[0, 4, :, pat].astype(F32) + v * sm).astype(BF16)

    def layer_two(rows):
        pre = jnp.dot(ker[1], cols(1, rows), preferred_element_type=F32)
        at = flat(*rows)
        v = pre[:C]
        s = jax.nn.sigmoid(pre[C:])
        g = dy[:, at] * (s * mk[1, :, at])
        delta = jnp.concatenate([g, g * v * (1.0 - s)], axis=0).astype(BF16)
        store_delta(1, rows, delta)

    def spread(layer, g):
        gpad[layer, :, :27 * C] = g
        for j in range(16):
            i, n = j // 4, j % 4
            gs[layer, j // tiles, j % tiles] = gpad[layer, i * 8:(i + 1) * 8, n * W:(n + 1) * W]

    def tally(ref, send_sem, recv_sem):
        return pltpu.make_async_remote_copy(
            src_ref=ref, dst_ref=ref, send_sem=send_sem, recv_sem=recv_sem,
            device_id={"ex": 1 - ex}, device_id_type=MESH)

    def rs_start(layer):
        def to(peer):
            return pltpu.make_async_remote_copy(
                src_ref=gs.at[layer, peer], dst_ref=rsr.at[ex, layer, mxy],
                send_sem=rs_s.at[layer], recv_sem=rs_r.at[ex, layer],
                device_id={"ex": 1, "slab": mz * gxy + peer}, device_id_type=MESH)

        for o in offs:
            to(xy_peer(o)).start()

        @pl.when(ex == 0)
        def _():
            to(mxy).start()

    def z_copy(group, o):
        at = pl.ds(*groups[group])
        return pltpu.make_async_remote_copy(
            src_ref=zr.at[mz, at], dst_ref=zr.at[mz, at],
            send_sem=z_s.at[group], recv_sem=z_r.at[group],
            device_id={"slab": lax.rem(mz + o, nz) * gxy + mxy}, device_id_type=MESH)

    def z_all(group):
        return tally(zr.at[pl.ds(1, nz - 1), pl.ds(*groups[group])], z_s.at[group], z_r.at[group])

    def ag_all(group, count):
        return tally(ag.at[pl.ds(0, count), pl.ds(*groups[group])], ag_s.at[group], ag_r.at[group])

    def ag_copy(group, o):
        at = pl.ds(*groups[group])
        return pltpu.make_async_remote_copy(
            src_ref=ag.at[mo, at], dst_ref=ag.at[mo, at],
            send_sem=ag_s.at[group], recv_sem=ag_r.at[group],
            device_id={"slab": mz * gxy + xy_peer(o)}, device_id_type=MESH)

    hand = pltpu.make_async_remote_copy(
        src_ref=kg_out, dst_ref=kg_out, send_sem=p_s, recv_sem=p_r,
        device_id={"ex": 1 - ex}, device_id_type=MESH)

    def rs_total(group):
        first_slot, count = groups[group]
        for q in range(first_slot, first_slot + count):
            e, layer = slots[q]
            if e == 1:
                rsr[1, layer, mxy] = gs[layer, mo]
            tally(rsr.at[e, layer, pl.ds(e, gxy - e)], rs_s.at[layer], rs_r.at[e, layer]).wait_recv()
            parts = [rsr[e, layer, r] for r in range(gxy)]
            while len(parts) > 1:
                parts = [a + b for a, b in zip(parts[::2], parts[1::2])]
            zr[mz, q] = parts[0]
        for o in zoffs:
            z_copy(group, o).start()

    def z_total(group):
        first_slot, count = groups[group]
        z_all(group).wait_recv()
        for q in range(first_slot, first_slot + count):
            parts = [zr[i, q] for i in range(nz)]
            while len(parts) > 1:
                parts = [a + b for a, b in zip(parts[::2], parts[1::2])]
            ag[mo, q] = parts[0]
        for o in offs:
            ag_copy(group, o).start()

    def input_grad():
        arrive(back_copy, 0, 0)
        for r in range(0, H, 8):
            rows = (r, r + 8)
            res = dy[:, flat(*rows)] + back_total(0, rows)
            for i in range(8):
                dx_out[:, r + i, :] = res[:, i * W:(i + 1) * W]

    for k in range(NC):
        arrive(halo_copy, 0, k)
        fill(0, 0, spans(0, k))
        fill(0, 2, spans(0, k))
        layer_one(spans(1, k))
        start(halo_copy, 1, k)
    fill(1, 1, (0, H))
    for k in range(NC):
        arrive(halo_copy, 1, k)
        fill(1, 0, spans(1, k))
        fill(1, 2, spans(1, k))
        layer_two(spans(2, k))
        back(1, spans(3, k))
        start(back_copy, 1, k)
    spread(1, weight_grad(1, (0, 16)) + weight_grad(1, (16, H)))
    g1 = None
    for k in range(NC):
        rows = spans(3, k)
        at = flat(*rows)
        arrive(back_copy, 1, k)
        dx = dy[:, at] + back_total(1, rows)
        dy[:, at] = dx
        delta = jnp.concatenate([dx * a1[:, at], dx * b1[:, at]], axis=0).astype(BF16)
        db[0, 1, :, flat(1 + rows[0], 1 + rows[1])] = delta
        part = weight_grad(0, rows)
        g1 = part if k == 0 else g1 + part
        if k == 1:
            rs_start(1)
    spread(0, g1)
    rs_start(0)
    for r in range(H):
        at = flat(1 + r, 2 + r)
        left, right = shifts(db[0, 1, :, at])
        db[0, 2, :, at] = left
        db[0, 0, :, at] = right
    for r in range(0, H, 16):
        back(0, (r, r + 16))
    start(back_copy, 0, 0)
    bound = 20.0 * float(depth * H * W) ** 0.5
    scaling = float(108 * C * C) ** 0.5 / (bound * 2.0 ** 0.5)

    def factor(e):
        square = None
        for q in range(4):
            if slots[q][0] == e:
                for j in range(16):
                    x = ag[j // tiles, q, j % tiles]
                    square = x * x if square is None else square + x * x
        norm = jnp.sqrt(jnp.sum(square, keepdims=True) + 1e-06)
        return jnp.minimum(1.0, bound / norm)

    @pl.when((ex == 1) & is_owner)
    def _():
        for group in range(len(groups)):
            rs_total(group)
        for group in range(len(groups)):
            z_total(group)

    @pl.when(ex == 1)
    def _():
        input_grad()

        @pl.when(is_owner)
        def _():
            for group in range(len(groups)):
                ag_all(group, held - 1).wait_recv()

        @pl.when(jnp.logical_not(is_owner))
        def _():
            for group in range(len(groups)):
                ag_all(group, held).wait_recv()

        factors = factor(0), factor(1)
        for layer in range(2):
            for j in range(16):
                i, n = j // 4, j % 4
                width = min(W, 27 * C - n * W)
                zero, one = (ag[j // tiles, slots.index((e, layer)), j % tiles] for e in range(2))
                both = (zero * factors[0] + one * factors[1]) * scaling
                kg_out[layer, i * 8:(i + 1) * 8, n * W:n * W + width] = both[:, :width]
        hand.start()
        @pl.when(is_owner)
        def _():
            for layer in range(2):
                tally(gs.at[layer, pl.ds(1, held - 1)], rs_s.at[layer], rs_r.at[1, layer]).wait_send()
            for group in range(len(groups)):
                z_all(group).wait_send()
                tally(ag.at[pl.ds(0, gxy - 1), pl.ds(*groups[group])], ag_s.at[group], ag_r.at[group]).wait_send()

        @pl.when(jnp.logical_not(is_owner))
        def _():
            for layer in range(2):
                tally(gs.at[layer], rs_s.at[layer], rs_r.at[1, layer]).wait_send()

        hand.wait_send()

    @pl.when(ex == 0)
    def _():
        input_grad()
        for layer in range(2):
            tally(gs.at[layer], rs_s.at[layer], rs_r.at[0, layer]).wait_send()
        hand.wait_recv()

    for layer in range(2):
        sent(layer)


def leave(dx_in, kg_in, dx_out, kg_out, sem):
    copies = [pltpu.make_async_copy(a, b, sem.at[i]) for i, (a, b) in enumerate(((dx_in, dx_out), (kg_in, kg_out)))]
    for copy in copies:
        copy.start()
    for copy in copies:
        copy.wait()


def in_hbm(x):
    return pltpu.with_memory_space_constraint(x, pltpu.HBM)


def per_device(volume, cotangent, gate_mask, loss_scale, canary, kernels):
    slabs = lax.axis_size("slab")
    torus = torus_of(slabs)
    nx, ny, nz = torus
    gxy = nx * ny
    held = len(owners_of(slabs))
    part = (16 // held, 8, W)
    sm = pl.BlockSpec(memory_space=pltpu.SMEM)
    hbm = pl.BlockSpec(memory_space=pltpu.HBM)
    anywhere = pl.BlockSpec(memory_space=pl.ANY)
    vm = pl.BlockSpec(memory_space=pltpu.VMEM)
    dma = pltpu.SemaphoreType.DMA
    shapes = (jax.ShapeDtypeStruct((C, H, W), F32), jax.ShapeDtypeStruct((2, 2 * C, 27 * C), F32))
    dx, kg = pl.pallas_call(
        functools.partial(kernel, torus, slabs),
        out_shape=shapes,
        in_specs=[hbm, hbm, hbm, sm, sm, hbm],
        out_specs=(vm, vm),
        scratch_shapes=[
            pltpu.VMEM((C, H, W), BF16),
            pltpu.VMEM((C, H, W), BF16),
            pltpu.VMEM((2, H, W), jnp.int32),
            pltpu.VMEM((2, 2 * C, 27 * C), BF16),
            pltpu.VMEM((C, H, W), F32),
            pltpu.VMEM((2, 9, C, PW), BF16),
            pltpu.VMEM((2, 3, 2 * C, PW), BF16),
            pltpu.VMEM((18 * C, W), F32),
            pltpu.VMEM((2, 3 * C, 18 * C), BF16),
            pltpu.VMEM((2, C, H * W), F32),
            pltpu.VMEM((C, H * W), F32),
            pltpu.VMEM((C, H * W), F32),
            pltpu.VMEM((C, H * W), F32),
            pltpu.VMEM((C, H * W), F32),
            pltpu.VMEM((2, 2, C, H * W), BF16),
            pltpu.VMEM((2, 2, C, H * W), BF16),
            pltpu.VMEM((2, 2 * C, 4 * W), F32),
            pltpu.VMEM((2, held) + part, F32),
            pltpu.VMEM((2, 2, gxy) + part, F32),
            pltpu.VMEM((nz, 4) + part, F32),
            pltpu.VMEM((held, 4) + part, F32),
            dma((2, 2)), dma((2, 2, NC)), dma((2, 2)), dma((2, NC + 1)),
            dma((2,)), dma((2, 2)), dma((3,)), dma((3,)), dma((3,)), dma((3,)),
            dma, dma, dma((4,)),
        ],
        compiler_params=pltpu.CompilerParams(
            collective_id=0, has_side_effects=True, vmem_limit_bytes=48 * 1024 * 1024),
        name="gated_level",
    )(
        in_hbm(volume.reshape((C, H, W))),
        in_hbm(cotangent.reshape((C, H, W))),
        in_hbm(gate_mask.reshape((2, H, W))),
        loss_scale,
        canary,
        in_hbm(kernels),
    )
    dx, kg = pl.pallas_call(
        leave,
        out_shape=shapes,
        in_specs=[anywhere, anywhere],
        out_specs=(hbm, hbm),
        scratch_shapes=[dma((2,))],
        compiler_params=pltpu.CompilerParams(vmem_limit_bytes=1024 * 1024),
        name="leave",
    )(dx, kg)
    return dx.reshape((1, C, 1, H, W)), kg


def solution(mesh):
    placed = (
        P("ex", None, "slab", None, None),
        P("ex", None, "slab", None, None),
        P("ex", None, "slab", None, None),
        P("ex"),
        P("ex"),
        P(),
    )
    return jax.shard_map(
        per_device,
        mesh=mesh,
        in_specs=placed,
        out_specs=(P("ex", None, "slab", None, None), P()),
        check_vma=False,
    )
```
